32 devices in a mesh: tm: 4 (over z), chan: 8 (over y, x, core).
Axes of the slice: x: 2, y: 2, z: 4, core: 2. Of those that a mesh axis runs over, the one named last changes fastest.
Arguments:
- voltages: bfloat16 [512, 1024, 1024], P('chan', None, 'tm'), may hold values from -4 to 4
- exponents: int32 [512, 16, 4], P('chan', None, 'tm'), may hold values from -2 to 2
- gain_real: float32 [512, 1024], P(None, 'chan'), may hold values from 0.1 to 1.9
- gain_imag: float32 [512, 1024], P(None, 'chan'), may hold values from -1.5 to 1.5
- delays: float32 [512, 256], replicated, may hold values from -8 to 8
- filter_taps: float32 [4, 1024], replicated, may hold values from -3 to 3
Outputs:
- beam_series: bfloat16 [256, 1024, 1024], P('chan', None, 'tm')
The draws below stay inside these ranges and needn't reach their ends.
All inputs are finite; a program needn't handle non-finite values.
Results may differ from the reference program's by a relative error of at most 0.0062.
Values may be sent and summed in bfloat16 or wider, within the bound.
A program may use at most 320 MiB of HBM per device.

```python
import math
import jax
import jax.numpy as jnp
from jax import lax

S = 512
C = 1024
B = 256
TAPS = 4
CB = 64
F_DEV = 128
GROUPS = 4
NF = 512
SCALE_BLOCKS = 16
N_TM = 4


def set_ends(result, rng, low, high):
    spot = [jax.random.randint(jax.random.fold_in(rng, axis), (), 0, length) for axis, length in enumerate(result.shape)]
    longest = result.shape.index(max(result.shape))
    next_to = spot[:longest] + [(spot[longest] + 1) % result.shape[longest]] + spot[longest + 1:]
    return result.at[tuple(spot)].set(low).at[tuple(next_to)].set(high)


def steps_of(rng, dims, cuts, low, top_value):
    loudness, own = 1.0, jax.random.fold_in(rng, 6)
    for dim, shards_of in cuts:
        heights = jnp.exp(jax.random.uniform(jax.random.fold_in(own, dim), (shards_of,), jnp.float32, low / len(cuts), top_value / len(cuts)))
        loudness = loudness * jnp.repeat(heights, dims[dim] // shards_of).reshape([-1 if axis == dim else 1 for axis in range(len(dims))])
    return loudness


def scatter_about(rng, dims, deviation, bound, split=(), kind=jnp.bfloat16):
    drawn = deviation * jax.random.normal(rng, dims, jnp.float32)
    if split:
        drawn = drawn * steps_of(rng, dims, split, -0.22, 0.18)
    return jnp.clip(drawn, -bound, bound).astype(kind)


def setup_inputs(seed: int = 0) -> dict:
    seeds = jax.random.split(jax.random.key(seed), 7)
    return {
        "voltages": scatter_about(seeds[0], (S, C, 2 * NF), 1.0, 4.0, ((0, 8), (2, 4))),
        "exponents": set_ends(jax.random.randint(seeds[1], (S, SCALE_BLOCKS, GROUPS), -2, 3), jax.random.fold_in(seeds[1], 1), -2, 2).astype(jnp.int32),
        "gain_real": jnp.clip(1.0 + 0.18 * jax.random.normal(seeds[2], (S, C), jnp.float32), 0.1, 1.9),
        "gain_imag": scatter_about(seeds[3], (S, C), 0.3, 1.5, ((1, 8),), jnp.float32),
        "delays": jnp.clip(jax.random.uniform(seeds[4], (S, B), jnp.float32, -8.0, 8.0), -8.0, 8.0),
        "filter_taps": scatter_about(seeds[5], (TAPS, C), 0.5, 3.0, (), jnp.float32),
    }


TWO_PI = 6.283185307179586

def inverse_tables(length):
    row_index = lax.broadcasted_iota(jnp.int32, (length, length), 0)
    col_index = lax.broadcasted_iota(jnp.int32, (length, length), 1)
    phases = TWO_PI / length * (row_index * col_index % length).astype(jnp.float32)
    normalizer = 1.0 / math.sqrt(length)
    cosine_table = (jnp.cos(phases) * normalizer).astype(jnp.bfloat16)
    sine_table = (jnp.sin(phases) * normalizer).astype(jnp.bfloat16)
    return (cosine_table, sine_table)

def reference(voltages, exponents, gain_real, gain_imag, delays, filter_taps):
    stations = voltages.shape[0]
    beam_count = delays.shape[1]
    scale_factor = 1.0 / math.sqrt(stations)
    cosine_table, sine_table = inverse_tables(C)

    def one_channel(channel_index):
        samples = lax.dynamic_index_in_dim(voltages, channel_index, 1, keepdims=False)
        exponent_row = lax.dynamic_index_in_dim(exponents, channel_index // CB, 1, keepdims=False)
        factor = jnp.exp2(exponent_row.astype(jnp.float32)).astype(jnp.bfloat16)
        scaled = (samples.reshape(stations, N_TM, 2 * F_DEV) * factor[:, :, None]).reshape(stations, 2 * NF)
        frequency = (channel_index.astype(jnp.float32) + 0.5) / C - 0.5
        phases = TWO_PI * frequency * jnp.transpose(delays)
        cosines = jnp.cos(phases)
        sines = jnp.sin(phases)
        real_gain = lax.dynamic_index_in_dim(gain_real, channel_index, 1, keepdims=False)[None, :]
        imag_gain = lax.dynamic_index_in_dim(gain_imag, channel_index, 1, keepdims=False)[None, :]
        weight_real = (real_gain * cosines + imag_gain * sines) * scale_factor
        weight_imag = (imag_gain * cosines - real_gain * sines) * scale_factor
        weights = jnp.concatenate([weight_real, weight_imag], axis=0).astype(jnp.bfloat16)
        product = jnp.dot(weights, scaled, preferred_element_type=jnp.float32).reshape(2 * beam_count, N_TM, 2, F_DEV)
        real_part = product[:beam_count, :, 0] - product[beam_count:, :, 1]
        imag_part = product[:beam_count, :, 1] + product[beam_count:, :, 0]
        return jnp.stack([real_part, imag_part], axis=2).astype(jnp.bfloat16)
    beams = lax.map(one_channel, jnp.arange(C, dtype=jnp.int32))
    tail_length = filter_taps.shape[0] - 1

    def one_beam(beam_index):
        spectra = lax.dynamic_index_in_dim(beams, beam_index, 1, keepdims=False).reshape(C, 2 * NF)
        cosine_part = jnp.dot(jnp.transpose(cosine_table), spectra, preferred_element_type=jnp.float32).reshape(C, N_TM, 2, F_DEV)
        sine_part = jnp.dot(jnp.transpose(sine_table), spectra, preferred_element_type=jnp.float32).reshape(C, N_TM, 2, F_DEV)
        real_part = cosine_part[:, :, 0] - sine_part[:, :, 1]
        imag_part = sine_part[:, :, 0] + cosine_part[:, :, 1]
        signal = jnp.stack([real_part, imag_part], axis=1).reshape(C, 2, NF)
        extended = jnp.concatenate([jnp.zeros((C, 2, tail_length), jnp.float32), signal], axis=2)
        running = jnp.zeros((C, 2, NF), jnp.float32)
        for tap_index in range(filter_taps.shape[0]):
            begin = tail_length - tap_index
            running = running + filter_taps[tap_index][:, None, None] * extended[:, :, begin:begin + NF]
        packed = jnp.transpose(running.reshape(C, 2, N_TM, F_DEV), (0, 2, 1, 3)).reshape(C, 2 * NF)
        return packed.astype(jnp.bfloat16)
    return lax.map(one_beam, jnp.arange(beam_count, dtype=jnp.int32))
```

```python
import functools
import math

import jax
import jax.numpy as jnp
from jax import lax
from jax.experimental import pallas as pl
from jax.experimental.pallas import tpu as pltpu
from jax.sharding import PartitionSpec as P

TWO_PI = 6.283185307179586
SETS = 2
QUAD = 4
VMEM_LIMIT = 60 * 1024 * 1024


def radix_of(chunk_channels):
    return max(r for r in (4, 2, 1) if chunk_channels % r == 0 and (chunk_channels // r) % 16 == 0 or r == 1)


def chip_grid(devices):
    cores = 2 if devices % 2 == 0 else 1
    chips = devices // cores
    rows = max(r for r in range(1, chips + 1) if chips % r == 0 and r * r <= chips)
    return rows, chips // rows, cores


def synthesis_tables(channels, devices, chunk_channels, radix):
    span = channels // radix
    per = chunk_channels // radix
    local = SETS * chunk_channels
    shape = (radix, span, span)
    residue = lax.broadcasted_iota(jnp.int32, shape, 0)
    sample = lax.broadcasted_iota(jnp.int32, shape, 1)
    place = lax.broadcasted_iota(jnp.int32, shape, 2)
    chunk = place // (devices * per)
    source = place // per % devices
    channel = source * local + chunk * chunk_channels + place % per * radix + residue
    phases = TWO_PI / channels * (channel * sample % channels).astype(jnp.float32)
    normalizer = 1.0 / math.sqrt(channels)
    cosine = (jnp.cos(phases) * normalizer).astype(jnp.bfloat16)
    sine = (jnp.sin(phases) * normalizer).astype(jnp.bfloat16)
    return jnp.concatenate([cosine, sine], axis=2)


class Side:
    def __init__(self, which, grid):
        self.rows, self.cols, self.cores = grid
        self.which = which
        self.group, self.reduce = (self.rows, self.cols) if which == 0 else (self.cols, self.rows)
        self.slots = self.group * self.cores

    def device(self, e, r, k):
        i, j = (e, r) if self.which == 0 else (r, e)
        return (i * self.cols + j) * self.cores + k

    def place(self):
        d = lax.axis_index("chan")
        k = d % self.cores
        j = d // self.cores % self.cols
        i = d // (self.cores * self.cols)
        return (i, j, k) if self.which == 0 else (j, i, k)

    def peer(self, off):
        e, r, k = self.place()
        e2 = (e + off // self.cores) % self.group
        k2 = (k + off % self.cores) % self.cores
        return e2 * self.cores + k2, self.device(e2, r, k2), e2, k2


def exchange_kernel(grid, n_taps, channels, radix, *refs):
    sides = [Side(s, grid) for s in range(SETS)]
    v = refs[0]
    gains, factors, delays = refs[1:3], refs[3:5], refs[5:7]
    spec, halo, raw, part, got, done, ends = (refs[7 + 2 * n : 9 + 2 * n] for n in range(7))
    scratch = refs[21:]
    xv, xf_re, xf_im, w_re, w_im, st_c, st_s = scratch[:7]
    s_re, s_im, ob, pa, pb, hal, hb, zero = scratch[7:15]
    gbuf, fbuf, fsum, rot_c, rot_s, dv = (scratch[15 + 2 * n : 17 + 2 * n] for n in range(6))
    raw_s, raw_r, gain_s, gain_r, fac_s, fac_r, part_s, part_r, fin_s, fin_r, end_s, end_r, loc, out_sem, in_sem = scratch[27:]

    per_station, _, lanes = v.shape
    half = lanes // 2
    devices = spec[0].shape[0]
    beams_local, h = spec[0].shape[1:3]
    beams = devices * beams_local
    local = channels // devices
    stations = st_c.shape[1]
    per = h // radix
    tail = n_taps - 1
    groups = lax.axis_size("tm")
    tm = lax.axis_index("tm")
    block = ob.shape[1]
    width = channels // fsum[0].shape[0]
    me = lax.axis_index("chan")

    bar = pltpu.get_barrier_semaphore()
    a, b = sides

    def greet(time, own):
        if own:
            pl.semaphore_signal(bar, inc=1, device_id={"tm": time, "chan": me})
        for off in range(1, a.slots):
            pl.semaphore_signal(bar, inc=1, device_id={"tm": time, "chan": a.peer(off)[1]})
        for off in range(b.cores, b.slots):
            pl.semaphore_signal(bar, inc=1, device_id={"tm": time, "chan": b.peer(off)[1]})

    friends = a.slots - 1 + b.slots - b.cores
    greet(tm, False)

    @pl.when(tm > 0)
    def _():
        greet(tm - 1, True)

    @pl.when(tm < groups - 1)
    def _():
        pl.semaphore_wait(bar, 2 * friends + 1)

    @pl.when(tm == groups - 1)
    def _():
        pl.semaphore_wait(bar, friends)

    def raw_copy(side, u, off):
        s = side.which
        e, r, k = side.place()
        _, device, e2, k2 = side.peer(off)
        start = pl.multiple_of(side.device(e2, u, k2) * local + s * h, h)
        return pltpu.make_async_remote_copy(
            v.at[:, pl.ds(start, h), :],
            raw[s].at[u, e * side.cores + k],
            raw_s.at[s, u, off],
            raw_r.at[s, u, off],
            device_id={"chan": device},
        )

    def gain_copy(side, d):
        s = side.which
        e, r, k = side.place()
        r2 = (r + d) % side.reduce
        return pltpu.make_async_remote_copy(
            gains[s].at[r2],
            gbuf[s].at[r],
            gain_s.at[s, d],
            gain_r.at[s, d],
            device_id={"chan": side.device(e, r2, k)},
        )

    def factor_copy(side, off):
        s = side.which
        e, r, k = side.place()
        return pltpu.make_async_remote_copy(
            factors[s],
            fbuf[s].at[e * side.cores + k],
            fac_s.at[s, off],
            fac_r.at[s, off],
            device_id={"chan": side.peer(off)[1]},
        )

    def part_copy(side, u, d):
        s = side.which
        e, r, k = side.place()
        r2 = (r + d) % side.reduce
        return pltpu.make_async_remote_copy(
            part[s].at[u, r2],
            got[s].at[u, r],
            part_s.at[s, u, d],
            part_r.at[s, u, d],
            device_id={"chan": side.device(e, r2, k)},
        )

    def final_copy(side, u, off):
        s = side.which
        e, r, k = side.place()
        q, device, _, _ = side.peer(off)
        return pltpu.make_async_remote_copy(
            done[s].at[u, q],
            spec[s].at[side.device(e, u, k)],
            fin_s.at[s, u, off],
            fin_r.at[s, u, off],
            device_id={"chan": device},
        )

    def end_copy(side, u, off):
        s = side.which
        e, r, k = side.place()
        q, device, _, _ = side.peer(off)
        return pltpu.make_async_remote_copy(
            ends[s].at[u, q],
            halo[s].at[side.device(e, u, k)],
            end_s.at[s, u, off],
            end_r.at[s, u, off],
            device_id={"tm": jnp.minimum(tm + 1, groups - 1), "chan": device},
        )

    for side in sides:
        for off in range(1, side.slots):
            factor_copy(side, off).start()
        for d in range(1, side.reduce):
            gain_copy(side, d).start()
    for u in range(max(side.reduce for side in sides)):
        for side in sides:
            if u < side.reduce:
                for off in range(side.cores, side.slots):
                    raw_copy(side, u, off).start()
                for off in range(1, side.cores):
                    raw_copy(side, u, off).start()

    for side in sides:
        s = side.which
        e, r, k = side.place()
        copies = [
            pltpu.make_async_copy(gains[s].at[r], gbuf[s].at[r], loc.at[0]),
            pltpu.make_async_copy(factors[s], fbuf[s].at[e * side.cores + k], loc.at[1]),
            pltpu.make_async_copy(delays[s], dv[s], loc.at[2]),
        ]
        for copy in copies:
            copy.start()
        for copy in copies:
            copy.wait()

        def rotate(n, carry, s=s):
            at = pl.ds(pl.multiple_of(n * 16, 16), 16)
            angle = (TWO_PI / channels) * dv[s][at, :]
            rot_c[s][at, :] = jnp.cos(angle)
            rot_s[s][at, :] = jnp.sin(angle)
            return carry

        lax.fori_loop(0, beams // 16, rotate, 0)
    zero[...] = jnp.zeros_like(zero)

    @pl.when(tm == 0)
    def _():
        for s in range(SETS):
            for d in range(devices):
                pltpu.make_async_copy(zero, halo[s].at[d], loc.at[0]).start()
                pltpu.make_async_copy(zero, halo[s].at[d], loc.at[0]).wait()

    for side in sides:
        s = side.which
        for off in range(1, side.slots):
            factor_copy(side, off).wait_recv()
        for d in range(1, side.reduce):
            gain_copy(side, d).wait_recv()
        total = fbuf[s][0]
        for q in range(1, side.slots):
            total = total + fbuf[s][q]
        fsum[s][...] = total

    def form(side, u):
        s = side.which
        e, r, k = side.place()
        first = side.device(e, u, k) * local + s * h
        loads = []
        for off in range(side.slots):
            q = side.peer(off)[0]
            if off == 0:
                source = v.at[:, pl.ds(pl.multiple_of(first, h), h), :]
            else:
                raw_copy(side, u, off).wait_recv()
                source = raw[s].at[u, q]
            loads.append(pltpu.make_async_copy(source, xv.at[pl.ds(q * per_station, per_station)], in_sem.at[off]))
            loads[-1].start()

        turns = TWO_PI * ((first.astype(jnp.float32) + 0.5) / channels - 0.5)

        def begin(n, carry):
            at = pl.ds(pl.multiple_of(n * 16, 16), 16)
            angle = turns * dv[s][at, :]
            st_c[at, :] = jnp.cos(angle)
            st_s[at, :] = jnp.sin(angle)
            return carry

        lax.fori_loop(0, beams // 16, begin, 0)
        for load in loads:
            load.wait()

        def tile(t, carry):
            def spread(n, carry):
                x = xv[pl.ds(pl.multiple_of(n * 16, 16), 16), pl.ds(pl.multiple_of(t * 16, 16), 16), :]
                x = x.astype(jnp.float32).reshape(256, lanes)
                at = pl.ds(pl.multiple_of(n * 256, 256), 256)
                xf_re[at, :] = x[:, :half]
                xf_im[at, :] = x[:, half:]
                return carry

            lax.fori_loop(0, stations // 16, spread, 0)

            def quad(g, carry):
                c0 = t * 16 + g * QUAD
                rows = []
                for q in range(QUAD):
                    scale = fsum[s][pl.ds((first + c0 + q) // width, 1), :]
                    rows.append((gbuf[s][u, 0, pl.ds(c0 + q, 1), :] * scale, gbuf[s][u, 1, pl.ds(c0 + q, 1), :] * scale))

                def weigh(n, carry):
                    at = pl.ds(pl.multiple_of(n * 16, 16), 16)
                    c, d = st_c[at, :], st_s[at, :]
                    rc, rs = rot_c[s][at, :], rot_s[s][at, :]
                    for q in range(QUAD):
                        gr, gi = rows[q]
                        w_re[q, at, :] = (gr * c + gi * d).astype(jnp.bfloat16)
                        w_im[q, at, :] = (gi * c - gr * d).astype(jnp.bfloat16)
                        c, d = c * rc - d * rs, d * rc + c * rs
                    st_c[at, :], st_s[at, :] = c, d
                    return carry

                lax.fori_loop(0, beams // 16, weigh, 0)
                for q in range(QUAD):
                    from_rows = pl.ds(g * QUAD + q, stations, stride=16)
                    x = jnp.concatenate([xf_re[from_rows, :], xf_im[from_rows, :]], axis=1).astype(jnp.bfloat16)
                    real = jnp.dot(w_re[q], x, preferred_element_type=jnp.float32)
                    imag = jnp.dot(w_im[q], x, preferred_element_type=jnp.float32)
                    c = c0 + q
                    to_rows = pl.ds(c % radix * per + c // radix, beams, stride=h)
                    s_re[to_rows, :] = real[:, :half] - imag[:, half:]
                    s_im[to_rows, :] = real[:, half:] + imag[:, :half]
                return carry

            lax.fori_loop(0, 16 // QUAD, quad, 0)
            return carry

        lax.fori_loop(0, h // 16, tile, 0)

        held = side.slots * beams_local

        def put(n):
            to = part[s].at[u, n * block // held, pl.ds(n * block % held, block)]
            return pltpu.make_async_copy(ob.at[n % 2], to, out_sem.at[n % 2])

        def flush(n, carry):
            @pl.when(n >= 2)
            def _():
                put(n - 2).wait()

            at = pl.ds(pl.multiple_of(n * block * h, block * h), block * h)
            ob[n % 2, :, :, :half] = s_re[at, :].reshape(block, h, half).astype(ob.dtype)
            ob[n % 2, :, :, half:] = s_im[at, :].reshape(block, h, half).astype(ob.dtype)
            put(n).start()
            return carry

        lax.fori_loop(0, beams // block, flush, 0)
        for n in range(2):
            put(beams // block - 2 + n).wait()
        for d in range(1, side.reduce):
            part_copy(side, u, d).start()

    def settle(side, u):
        s = side.which
        e, r, k = side.place()
        slot = side.device(e, u, k)
        per_slot = beams_local // block
        lane = lax.broadcasted_iota(jnp.int32, (h, half), 1)
        for d in range(1, side.reduce):
            part_copy(side, u, d).wait_recv()

        def finish(off, own):
            q = side.peer(off)[0]

            def fetch(n):
                at = pl.ds(q * beams_local + n * block, block)
                copies = [pltpu.make_async_copy(part[s].at[u, r, at], pa.at[n % 2, 0], in_sem.at[n % 2 * side.reduce])]
                for d in range(1, side.reduce):
                    other = got[s].at[u, (r + d) % side.reduce, at]
                    copies.append(pltpu.make_async_copy(other, pa.at[n % 2, d], in_sem.at[n % 2 * side.reduce + d]))
                return copies

            def put(n):
                at = pl.ds(n * block, block)
                to = spec[s].at[slot, at] if own else done[s].at[u, q, at]
                return pltpu.make_async_copy(pb.at[n % 2], to, out_sem.at[n % 2])

            for copy in fetch(0):
                copy.start()
            hal[...] = jnp.zeros_like(hal)
            for n in range(per_slot):
                for copy in fetch(n):
                    copy.wait()
                if n + 1 < per_slot:
                    for copy in fetch(n + 1):
                        copy.start()
                if n >= 2:
                    put(n - 2).wait()

                def add(t, carry, n=n):
                    total = pa[n % 2, 0, t].astype(jnp.float32)
                    for d in range(1, side.reduce):
                        total = total + pa[n % 2, d, t].astype(jnp.float32)
                    pb[n % 2, t] = total.astype(pb.dtype)
                    first = n_taps * (n * block + t)
                    place = lane - first
                    keep = jnp.logical_and(place >= 0, place < tail)
                    for p in range(2):
                        cols = slice(p * half, (p + 1) * half)
                        moved = pltpu.roll(total[:, cols], (first + tail) % half, 1)
                        hal[:, cols] = jnp.where(keep, moved, hal[:, cols])
                    return carry

                lax.fori_loop(0, block, add, 0)
                put(n).start()
            for n in range(max(0, per_slot - 2), per_slot):
                put(n).wait()
            if not own:
                final_copy(side, u, off).start()

            @pl.when(tm < groups - 1)
            def _():
                hb[...] = hal[...].astype(hb.dtype)
                out = pltpu.make_async_copy(hb, ends[s].at[u, q], loc.at[1])
                out.start()
                out.wait()
                end_copy(side, u, off).start()

        def others(off, carry):
            finish(off, False)
            return carry

        lax.fori_loop(1, side.slots, others, 0)
        finish(0, True)

    def each(work):
        for u in range(max(side.reduce for side in sides)):
            for side in sides:
                if u < side.reduce:
                    work(side, u)

    def looped(work):
        if a.reduce != b.reduce:
            return each(work)

        def body(u, carry):
            for side in sides:
                work(side, u)
            return carry

        lax.fori_loop(0, a.reduce, body, 0)

    looped(form)
    looped(settle)

    for side in sides:
        for off in range(1, side.slots):
            factor_copy(side, off).wait_send()
        for d in range(1, side.reduce):
            gain_copy(side, d).wait_send()
        for u in range(side.reduce):
            for off in range(1, side.slots):
                raw_copy(side, u, off).wait_send()
                final_copy(side, u, off).wait()
            for d in range(1, side.reduce):
                part_copy(side, u, d).wait_send()

            @pl.when(tm < groups - 1)
            def _():
                for off in range(side.slots):
                    end_copy(side, u, off).wait_send()

            @pl.when(tm > 0)
            def _():
                for off in range(side.slots):
                    end_copy(side, u, off).wait_recv()


def exchange(voltages, gains, factors, delays, grid, devices, channels, radix, n_taps):
    per_station, _, lanes = voltages.shape
    half = lanes // 2
    sides = [Side(s, grid) for s in range(SETS)]
    beams = delays[0].shape[0]
    stations = delays[0].shape[1]
    beams_local = beams // devices
    h = channels // devices // SETS
    block = min(16, beams_local)
    most = max(side.slots for side in sides)
    deep = max(side.reduce for side in sides)
    bf, f32 = jnp.bfloat16, jnp.float32
    hbm = lambda *shape: jax.ShapeDtypeStruct(shape, bf)
    outs = [hbm(devices, beams_local, h, lanes)] * 2 + [hbm(devices, h, lanes)] * 2
    outs += [hbm(side.reduce, side.slots, per_station, h, lanes) for side in sides]
    outs += [hbm(side.reduce, side.reduce, side.slots * beams_local, h, lanes) for side in sides] * 2
    outs += [hbm(side.reduce, side.slots, beams_local, h, lanes) for side in sides]
    outs += [hbm(side.reduce, side.slots, h, lanes) for side in sides]
    any_space = pl.BlockSpec(memory_space=pl.ANY)
    vm = pltpu.VMEM
    blocks = factors[0].shape[0]
    scratch = [
        vm((stations, h, lanes), bf),
        vm((stations * 16, half), f32),
        vm((stations * 16, half), f32),
        vm((QUAD, beams, stations), bf),
        vm((QUAD, beams, stations), bf),
        vm((beams, stations), f32),
        vm((beams, stations), f32),
        vm((beams * h, half), f32),
        vm((beams * h, half), f32),
        vm((2, block, h, lanes), bf),
        vm((2, deep, block, h, lanes), bf),
        vm((2, block, h, lanes), bf),
        vm((h, lanes), f32),
        vm((h, lanes), bf),
        vm((h, lanes), bf),
    ]
    scratch += [vm((side.reduce, 2, h, stations), f32) for side in sides]
    scratch += [vm((side.slots, blocks, stations), f32) for side in sides]
    scratch += [vm((blocks, stations), f32) for _ in sides]
    scratch += [vm((beams, stations), f32)] * 6
    dma = pltpu.SemaphoreType.DMA
    scratch += [dma((SETS, deep, most))] * 2 + [dma((SETS, deep))] * 2 + [dma((SETS, most))] * 2
    scratch += [dma((SETS, deep, deep))] * 2 + [dma((SETS, deep, most))] * 4
    scratch += [dma((3,)), dma((2,)), dma((max(most, 2 * deep),))]
    results = pl.pallas_call(
        functools.partial(exchange_kernel, grid, n_taps, channels, radix),
        name="exchange",
        in_specs=[any_space] * 7,
        out_specs=[any_space] * len(outs),
        out_shape=outs,
        scratch_shapes=scratch,
        compiler_params=pltpu.CompilerParams(
            collective_id=0, has_side_effects=True, vmem_limit_bytes=VMEM_LIMIT
        ),
    )(voltages, *gains, *factors, *delays)
    return results[:2], results[2:4]


def times_unit(value, turn, radix):
    re, im = value
    quarter = turn * (4 // radix) % 4
    return ((re, im), (-im, re), (-re, -im), (im, -re))[quarter]


def combine(values, q):
    radix = len(values)
    re, im = values[0]
    for r in range(1, radix):
        more_re, more_im = times_unit(values[r], r * q, radix)
        re, im = re + more_re, im + more_im
    return re, im


def synthesis_kernel(radix, *refs):
    tab, taps_masked = refs[:2]
    blocks = refs[2 : 2 + SETS]
    halos = refs[2 + SETS : 2 + 2 * SETS]
    o, partial, before = refs[2 + 2 * SETS :]
    n_taps, channels, half = taps_masked.shape
    span = channels // radix
    rows = 16
    beam = pl.program_id(0)

    def transform(chunks, slot, r):
        per = chunks[0].shape[1] // radix
        parts = [c[:, r * per : (r + 1) * per, :].reshape(-1, 2 * half) for c in chunks]
        x = jnp.concatenate(parts, axis=0)
        turned = jnp.concatenate([-x[:, half:], x[:, :half]], axis=1)
        both = jnp.concatenate([x, turned], axis=0)
        partial[slot, r] = jnp.dot(tab[r], both, preferred_element_type=jnp.float32)

    def on_rows(start, slot, store):
        values = []
        for r in range(radix):
            both = partial[slot, r, pl.ds(start, rows), :]
            values.append((both[:, :half], both[:, half:]))
        for q in range(radix):
            store(pl.ds(q * span + start, rows), combine(values, q))

    lane = lax.broadcasted_iota(jnp.int32, (rows, half), 1)

    @pl.when(beam == 0)
    def _():
        for r in range(radix):
            transform(halos, 1, r)
        frame = lane % n_taps

        def store(at, signal):
            for part in range(2):
                total = jnp.zeros((rows, half), jnp.float32)
                for k in range(1, n_taps):
                    back = n_taps - 1 - k
                    moved = pltpu.roll(signal[part], (half - back) % half, 1) if back else signal[part]
                    tap = jnp.broadcast_to(taps_masked[k, at, :][:, half - 1 :], (rows, half))
                    total = total + jnp.where(frame < k, tap * moved, 0.0)
                before[at, part * half : (part + 1) * half] = total

        def body(i, carry):
            on_rows(pl.multiple_of(i * rows, rows), 1, store)
            return carry

        lax.fori_loop(0, span // rows, body, 0)

    new, old = beam % 2, (beam + 1) % 2
    shift = (half - n_taps * jnp.maximum(beam - 1, 0)) % half

    def store(at, signal):
        for part in range(2):
            cols = slice(part * half, (part + 1) * half)
            total = taps_masked[0, at, :] * signal[part]
            for k in range(1, n_taps):
                total = total + taps_masked[k, at, :] * pltpu.roll(signal[part], k, 1)
            total = total + jnp.where(lane < n_taps - 1, pltpu.roll(before[at, cols], shift, 1), 0.0)
            o[at, cols] = total.astype(o.dtype)

    for r in range(radix):
        transform(blocks, new, r)
        for start in range(r * span // radix, (r + 1) * span // radix, rows):
            on_rows(start, old, store)


def synthesize(tables, filter_taps, spectra, halos, radix):
    devices, beams, chunk_channels, lanes = spectra[0].shape
    n_taps, channels = filter_taps.shape
    half = lanes // 2
    span = channels // radix
    with jax.named_scope("taps"):
        taps = jnp.broadcast_to(filter_taps[:, :, None], (n_taps, channels, half))
        lane = lax.broadcasted_iota(jnp.int32, taps.shape, 2)
        masked = jnp.where(lane >= lax.broadcasted_iota(jnp.int32, taps.shape, 0), taps, 0.0)
    whole = lambda shape: pl.BlockSpec(shape, lambda b: (0,) * len(shape), pipeline_mode=pl.Buffered(1))
    return pl.pallas_call(
        functools.partial(synthesis_kernel, radix),
        name="synthesize",
        grid=(beams + 1,),
        in_specs=[whole(tables.shape), whole(taps.shape)]
        + [pl.BlockSpec((devices, None, chunk_channels, lanes), lambda b: (0, jnp.minimum(b, beams - 1), 0, 0))] * SETS
        + [whole(halos[0].shape)] * SETS,
        out_specs=pl.BlockSpec((None, channels, lanes), lambda b: (jnp.maximum(b - 1, 0), 0, 0)),
        out_shape=jax.ShapeDtypeStruct((beams, channels, lanes), jnp.bfloat16),
        scratch_shapes=[
            pltpu.VMEM((2, radix, span, lanes), jnp.float32),
            pltpu.VMEM((channels, lanes), jnp.float32),
        ],
        compiler_params=pltpu.CompilerParams(vmem_limit_bytes=56 * 1024 * 1024),
    )(tables, masked, *spectra, *halos)


def per_device(voltages, exponents, gain_real, gain_imag, delays, filter_taps):
    per_station, channels, lanes = voltages.shape
    devices = lax.axis_size("chan")
    local = channels // devices
    h = local // SETS
    radix = radix_of(h)
    beams = delays.shape[1]
    beams_local = beams // devices
    n_taps = filter_taps.shape[0]
    grid = chip_grid(devices)
    rows, cols, cores = grid
    n_stations = delays.shape[0]
    normalizer = 1.0 / math.sqrt(n_stations)
    factor = jnp.exp2(exponents[:, :, 0].astype(jnp.float32)).astype(jnp.bfloat16).astype(jnp.float32)
    gains, factors, angles = [], [], []
    for s in range(SETS):
        side = Side(s, grid)
        e, r, k = side.place()
        with jax.named_scope(f"prepare_{s}"):
            pair = []
            for gain in (gain_real, gain_imag):
                part = (gain[:, s * h : (s + 1) * h] * normalizer).reshape(rows, cols, cores * per_station, h)
                order = (1, 3, 0, 2) if s == 0 else (0, 3, 1, 2)
                pair.append(jnp.transpose(part, order).reshape(side.reduce, h, -1))
            gains.append(jnp.stack(pair, axis=1))
            here = lax.broadcasted_iota(jnp.int32, (1, side.slots, 1), 1) == e * cores + k
            placed = jnp.where(here, jnp.transpose(factor)[:, None, :], 0.0)
            factors.append(placed.reshape(factor.shape[1], side.slots * per_station))
            table = delays.reshape(rows, cols, cores * per_station, rows, cols, cores * beams_local)
            table = lax.dynamic_index_in_dim(table, r, 1 - s, keepdims=False)
            order = (3, 2, 4, 0, 1) if s == 0 else (2, 3, 4, 0, 1)
            angles.append(jnp.transpose(table, order).reshape(beams, side.slots * per_station))
    with jax.named_scope("exchange"):
        spectra, halos = exchange(voltages, gains, factors, angles, grid, devices, channels, radix, n_taps)
    with jax.named_scope("tables"):
        tables = synthesis_tables(channels, devices, h, radix)
    return synthesize(tables, filter_taps, spectra, halos, radix)


def solution(mesh):
    placed = (
        P("chan", None, "tm"),
        P("chan", None, "tm"),
        P(None, "chan"),
        P(None, "chan"),
        P(),
        P(),
    )
    return jax.shard_map(per_device, mesh=mesh, in_specs=placed, out_specs=P("chan", None, "tm"), check_vma=False)
```

```python
import functools
import math

import jax
import jax.numpy as jnp
from jax import lax
from jax.experimental import pallas as pl
from jax.experimental.pallas import tpu as pltpu
import numpy as np
from jax.sharding import PartitionSpec as P

TWO_PI = 6.283185307179586
SETS = 2
QUAD = 4
VMEM_LIMIT = 60 * 1024 * 1024


def radix_of(chunk_channels):
    return max(r for r in (4, 2, 1) if chunk_channels % r == 0 and (chunk_channels // r) % 16 == 0 or r == 1)


def chip_grid(devices):
    cores = 2 if devices % 2 == 0 else 1
    chips = devices // cores
    rows = max(r for r in range(1, chips + 1) if chips % r == 0 and r * r <= chips)
    return rows, chips // rows, cores


class Side:
    def __init__(self, which, grid):
        self.rows, self.cols, self.cores = grid
        self.which = which
        self.group, self.reduce = (self.rows, self.cols) if which == 0 else (self.cols, self.rows)
        self.slots = self.group * self.cores

    def device(self, e, r, k):
        i, j = (e, r) if self.which == 0 else (r, e)
        return (i * self.cols + j) * self.cores + k

    def place(self):
        d = lax.axis_index("chan")
        k = d % self.cores
        j = d // self.cores % self.cols
        i = d // (self.cores * self.cols)
        return (i, j, k) if self.which == 0 else (j, i, k)

    def peer(self, off):
        e, r, k = self.place()
        e2 = (e + off // self.cores) % self.group
        k2 = (k + off % self.cores) % self.cores
        return e2 * self.cores + k2, self.device(e2, r, k2), e2, k2


def exchange_kernel(grid, n_taps, channels, radix, *refs):
    sides = [Side(s, grid) for s in range(SETS)]
    v, factors, gains, dl, ft, base = refs[0], refs[1:3], refs[3:5], refs[5], refs[6], refs[7]
    out = refs[8]
    spec, raw, part, got, done = (refs[9 + 2 * n : 11 + 2 * n] for n in range(5))
    scratch = refs[19:]
    xv, xf_re, xf_im, w_re, w_im, st_c, st_s, s_re, s_im, ob = scratch[:10]
    tab, taps, partial, before, xin, oo, ftv, basev = scratch[10:18]
    pa, pb = scratch[18:20]
    pairs = (scratch[20 + 2 * n : 22 + 2 * n] for n in range(12))
    gt, gsel, gbuf, fbuf, fsum, dtmp, dv, rot_c, rot_s, hal, hb, hv = pairs
    sems = scratch[44:]
    raw_s, raw_r, gain_s, gain_r, fac_s, fac_r, part_s, part_r, fin_s, fin_r, end_s, end_r = sems[:12]
    gain_in, delay_in, extra_in, own_in, load_in, out_sem, fetch_in, put_sem, x_in, o_out = sems[12:]

    per_station, _, lanes = v.shape
    half = lanes // 2
    beams_local = spec[0].shape[1]
    devices, h = spec[0].shape[0], spec[0].shape[2]
    beams = devices * beams_local
    local = channels // devices
    stations = st_c.shape[1]
    per = h // radix
    span = channels // radix
    tail = n_taps - 1
    groups = lax.axis_size("tm")
    tm = lax.axis_index("tm")
    block = ob.shape[1]
    piece = beams_local // fin_s.shape[3]
    pieces = beams_local // piece
    early = max(1, 5 * pieces // 8)
    width = channels // fsum[0].shape[0]
    me = lax.axis_index("chan")
    rows, cols, cores = grid
    normalizer = 1.0 / math.sqrt(rows * cols * cores * per_station)

    bar = pltpu.get_barrier_semaphore()
    a, b = sides

    def greet(time, own):
        if own:
            pl.semaphore_signal(bar, inc=1, device_id={"tm": time, "chan": me})
        for off in range(1, a.slots):
            pl.semaphore_signal(bar, inc=1, device_id={"tm": time, "chan": a.peer(off)[1]})
        for off in range(b.cores, b.slots):
            pl.semaphore_signal(bar, inc=1, device_id={"tm": time, "chan": b.peer(off)[1]})

    friends = a.slots - 1 + b.slots - b.cores
    greet(tm, False)

    @pl.when(tm > 0)
    def _():
        greet(tm - 1, True)

    @pl.when(tm < groups - 1)
    def _():
        pl.semaphore_wait(bar, 2 * friends + 1)

    @pl.when(tm == groups - 1)
    def _():
        pl.semaphore_wait(bar, friends)

    def raw_copy(side, u, off):
        s = side.which
        e, r, k = side.place()
        _, device, e2, k2 = side.peer(off)
        start = pl.multiple_of(side.device(e2, u, k2) * local + s * h, h)
        return pltpu.make_async_remote_copy(
            v.at[:, pl.ds(start, h), :],
            raw[s].at[u, e * side.cores + k],
            raw_s.at[s, u, off],
            raw_r.at[s, u, off],
            device_id={"chan": device},
        )

    def gain_copy(side, d):
        s = side.which
        e, r, k = side.place()
        r2 = (r + d) % side.reduce
        return pltpu.make_async_remote_copy(
            gsel[s].at[r2],
            gbuf[s].at[r],
            gain_s.at[s, d],
            gain_r.at[s, d],
            device_id={"chan": side.device(e, r2, k)},
        )

    def factor_copy(side, off):
        s = side.which
        e, r, k = side.place()
        return pltpu.make_async_remote_copy(
            factors[s],
            fbuf[s].at[e * side.cores + k],
            fac_s.at[s, off],
            fac_r.at[s, off],
            device_id={"chan": side.peer(off)[1]},
        )

    def part_copy(side, u, d):
        s = side.which
        e, r, k = side.place()
        r2 = (r + d) % side.reduce
        return pltpu.make_async_remote_copy(
            part[s].at[u, r2],
            got[s].at[u, r],
            part_s.at[s, u, d],
            part_r.at[s, u, d],
            device_id={"chan": side.device(e, r2, k)},
        )

    def final_copy(side, u, off, g):
        s = side.which
        e, r, k = side.place()
        q, device, _, _ = side.peer(off)
        at = pl.ds(g * piece, piece)
        return pltpu.make_async_remote_copy(
            done[s].at[u, q, at],
            spec[s].at[side.device(e, u, k), at],
            fin_s.at[s, u, off, g],
            fin_r.at[s, u, off, g],
            device_id={"chan": device},
        )

    def end_copy(side, u, off):
        s = side.which
        e, r, k = side.place()
        q, device, _, _ = side.peer(off)
        return pltpu.make_async_remote_copy(
            hb[s].at[u, q],
            hv[s].at[side.device(e, u, k)],
            end_s.at[s, u, off],
            end_r.at[s, u, off],
            device_id={"tm": jnp.minimum(tm + 1, groups - 1), "chan": device},
        )

    def span_of(side, source, r):
        return source.at[:, r] if side.which == 0 else source.at[r]

    def start_raw(u):
        for side in sides:
            if u < side.reduce:
                for off in range(side.cores, side.slots):
                    raw_copy(side, u, off).start()
                for off in range(1, side.cores):
                    raw_copy(side, u, off).start()

    def loop(low, high, work):
        def body(n, carry):
            work(n)
            return carry

        lax.fori_loop(low, high, body, 0)

    def aligned(n, size):
        return pl.ds(pl.multiple_of(n * size, size), size)

    start_raw(0)
    gain_loads, delay_loads, extra_loads, own_loads = [], [], [], []
    for side in sides:
        s = side.which
        e, r, k = side.place()
        for off in range(1, side.slots):
            factor_copy(side, off).start()
        for r2 in range(side.reduce):
            for p in range(2):
                source = span_of(side, gains[p], r2)
                gain_loads.append(pltpu.make_async_copy(source, gt[s].at[r2, p], gain_in.at[s, r2, p]))
        delay_loads.append(pltpu.make_async_copy(span_of(side, dl, r), dtmp[s], delay_in.at[s]))
        own_loads.append(pltpu.make_async_copy(factors[s], fbuf[s].at[e * side.cores + k], own_in.at[s]))
    extra_loads = [pltpu.make_async_copy(ft, ftv, extra_in.at[0]), pltpu.make_async_copy(base, basev, extra_in.at[1])]
    loads = gain_loads + delay_loads + own_loads + extra_loads
    for load in loads:
        load.start()
    for load in loads:
        load.wait()
    for side in sides:
        s = side.which
        for r2 in range(side.reduce):
            for p in range(2):
                turned = jnp.transpose(gt[s][r2, p].reshape(stations, local))
                gsel[s][r2, p] = turned[s * h : (s + 1) * h] * normalizer
    for side in sides:
        s = side.which
        turned = jnp.transpose(dtmp[s][...].reshape(stations, beams))
        held = cores * beams_local
        for i in range(rows):
            for j in range(cols):
                e, r = (i, j) if s == 0 else (j, i)
                to = (r * side.group + e) * held
                at = (i * cols + j) * held
                dv[s][to : to + held, :] = turned[at : at + held]
    for side in sides:
        for d in range(1, side.reduce):
            gain_copy(side, d).start()
    for u in range(1, max(side.reduce for side in sides)):
        start_raw(u)

    for side in sides:
        s = side.which
        r = side.place()[1]
        gbuf[s][r] = gsel[s][r]

        def rotate(n, s=s):
            at = aligned(n, 16)
            angle = (TWO_PI / channels) * dv[s][at, :]
            rot_c[s][at, :] = jnp.cos(angle)
            rot_s[s][at, :] = jnp.sin(angle)

        loop(0, beams // 16, rotate)
    for r in range(radix):

        def tabulate(n, r=r):
            at = aligned(n, 16)
            sample = n * 16 + lax.broadcasted_iota(jnp.int32, (16, span), 0)
            product = sample * (basev[0:1, :] + r)
            product = product & (channels - 1) if channels & (channels - 1) == 0 else lax.rem(product, channels)
            phases = TWO_PI / channels * product.astype(jnp.float32)
            tab[r, at, :span] = (jnp.cos(phases) * (1.0 / math.sqrt(channels))).astype(tab.dtype)
            tab[r, at, span:] = (jnp.sin(phases) * (1.0 / math.sqrt(channels))).astype(tab.dtype)

        loop(0, span // 16, tabulate)

    def spread_taps(n):
        at = aligned(n, half)
        lane = lax.broadcasted_iota(jnp.int32, (half, half), 1)
        for k in range(n_taps):
            column = jnp.transpose(jnp.broadcast_to(ftv[k : k + 1, at], (half, half)))
            taps[k, at, :] = jnp.where(lane >= k, column, 0.0)

    loop(0, channels // half, spread_taps)
    for side in sides:
        s = side.which
        hal[s][...] = jnp.zeros_like(hal[s])
        for off in range(1, side.slots):
            factor_copy(side, off).wait_recv()
        for d in range(1, side.reduce):
            gain_copy(side, d).wait_recv()
        total = fbuf[s][0]
        for q in range(1, side.slots):
            total = total + fbuf[s][q]
        fsum[s][...] = total

    @pl.when(tm == 0)
    def _():
        for s in range(SETS):
            hv[s][...] = jnp.zeros_like(hv[s])

    def form(side, u):
        s = side.which
        e, r, k = side.place()
        first = side.device(e, u, k) * local + s * h
        loads = []
        for off in range(side.slots):
            q = side.peer(off)[0]
            if off == 0:
                source = v.at[:, pl.ds(pl.multiple_of(first, h), h), :]
            else:
                raw_copy(side, u, off).wait_recv()
                source = raw[s].at[u, q]
            loads.append(pltpu.make_async_copy(source, xv.at[pl.ds(q * per_station, per_station)], load_in.at[off]))
            loads[-1].start()

        turns = TWO_PI * ((first.astype(jnp.float32) + 0.5) / channels - 0.5)

        def begin(n):
            at = aligned(n, 16)
            angle = turns * dv[s][at, :]
            st_c[at, :] = jnp.cos(angle)
            st_s[at, :] = jnp.sin(angle)

        loop(0, beams // 16, begin)
        for load in loads:
            load.wait()

        def tile(t):
            def spread(n):
                x = xv[aligned(n, 16), aligned(t, 16), :]
                x = x.astype(jnp.float32).reshape(256, lanes)
                at = aligned(n, 256)
                xf_re[at, :] = x[:, :half]
                xf_im[at, :] = x[:, half:]

            loop(0, stations // 16, spread)

            def quad(g):
                c0 = t * 16 + g * QUAD
                pair = []
                for q in range(QUAD):
                    scale = fsum[s][pl.ds((first + c0 + q) // width, 1), :]
                    pair.append((gbuf[s][u, 0, pl.ds(c0 + q, 1), :] * scale, gbuf[s][u, 1, pl.ds(c0 + q, 1), :] * scale))

                def weigh(n):
                    at = aligned(n, 16)
                    c, d = st_c[at, :], st_s[at, :]
                    rc, rs = rot_c[s][at, :], rot_s[s][at, :]
                    for q in range(QUAD):
                        gr, gi = pair[q]
                        w_re[q, at, :] = (gr * c + gi * d).astype(jnp.bfloat16)
                        w_im[q, at, :] = (gi * c - gr * d).astype(jnp.bfloat16)
                        c, d = c * rc - d * rs, d * rc + c * rs
                    st_c[at, :], st_s[at, :] = c, d

                loop(0, beams // 16, weigh)
                for q in range(QUAD):
                    from_rows = pl.ds(g * QUAD + q, stations, stride=16)
                    x = jnp.concatenate([xf_re[from_rows, :], xf_im[from_rows, :]], axis=1).astype(jnp.bfloat16)
                    real = jnp.dot(w_re[q], x, preferred_element_type=jnp.float32)
                    imag = jnp.dot(w_im[q], x, preferred_element_type=jnp.float32)
                    c = c0 + q
                    to_rows = pl.ds(c % radix * per + c // radix, beams, stride=h)
                    s_re[to_rows, :] = real[:, :half] - imag[:, half:]
                    s_im[to_rows, :] = real[:, half:] + imag[:, :half]

            loop(0, 16 // QUAD, quad)

        loop(0, h // 16, tile)

        held = side.slots * beams_local

        def put(n):
            to = part[s].at[u, n * block // held, pl.ds(n * block % held, block)]
            return pltpu.make_async_copy(ob.at[n % 2], to, out_sem.at[n % 2])

        def flush(n):
            @pl.when(n >= 2)
            def _():
                put(n - 2).wait()

            at = aligned(n, block * h)
            ob[n % 2, :, :, :half] = s_re[at, :].reshape(block, h, half).astype(ob.dtype)
            ob[n % 2, :, :, half:] = s_im[at, :].reshape(block, h, half).astype(ob.dtype)
            put(n).start()

        loop(0, beams // block, flush)
        for n in range(2):
            put(beams // block - 2 + n).wait()
        for d in range(1, side.reduce):
            part_copy(side, u, d).start()

    def settle(side, u, send):
        s = side.which
        e, r, k = side.place()
        slot = side.device(e, u, k)
        lane = lax.broadcasted_iota(jnp.int32, (h, half), 1)
        ahead = pa.shape[0] - 1
        count = beams_local // block * side.slots
        for d in range(1, side.reduce):
            part_copy(side, u, d).wait_recv()

        def where_of(n):
            return side.peer(n % side.slots)[0], n // side.slots

        def fetch(n):
            q, g = where_of(n)
            at = pl.ds(q * beams_local + g * block, block)
            now = n % (ahead + 1)
            copies = [pltpu.make_async_copy(part[s].at[u, r, at], pa.at[now, 0], fetch_in.at[now, 0])]
            for d in range(1, side.reduce):
                other = got[s].at[u, (r + d) % side.reduce, at]
                copies.append(pltpu.make_async_copy(other, pa.at[now, d], fetch_in.at[now, d]))
            return copies

        def put(n, own):
            q, g = where_of(n)
            at = pl.ds(g * block, block)
            to = spec[s].at[slot, at] if own else done[s].at[u, q, at]
            return pltpu.make_async_copy(pb.at[n % 2], to, put_sem.at[n % 2])

        def pass_on(n):
            put(n, False).wait()
            if send:
                for g in range(block // piece):
                    at = n // side.slots * (block // piece) + g

                    @pl.when(jnp.logical_and(n % side.slots > 0, at < early))
                    def _(at=at):
                        final_copy(side, u, n % side.slots, at).start()

        for n in range(min(ahead, count)):
            for copy in fetch(n):
                copy.start()

        def step(n):
            q, g = where_of(n)
            now = n % (ahead + 1)
            for copy in fetch(n):
                copy.wait()

            @pl.when(n + ahead < count)
            def _():
                for copy in fetch(n + ahead):
                    copy.start()

            def add(t):
                total = pa[now, 0, t].astype(jnp.float32)
                for d in range(1, side.reduce):
                    total = total + pa[now, d, t].astype(jnp.float32)
                pb[n % 2, t] = total.astype(pb.dtype)
                first = n_taps * (g * block + t)
                place = lane - first
                keep = jnp.logical_and(place >= 0, place < tail)
                for p in range(2):
                    at = slice(p * half, (p + 1) * half)
                    moved = pltpu.roll(total[:, at], (first + tail) % half, 1)
                    hal[s][u, q, :, at] = jnp.where(keep, moved, hal[s][u, q, :, at])

            def add_pair(t):
                add(2 * t)
                add(2 * t + 1)

            loop(0, block // 2, add_pair)

            @pl.when(n > 0)
            def _():
                pass_on(n - 1)

            @pl.when(n % side.slots == 0)
            def _():
                put(n, True).start()

            @pl.when(n % side.slots > 0)
            def _():
                put(n, False).start()

        loop(0, count, step)
        pass_on(count - 1)
        hb[s][u] = hal[s][u].astype(hb[s].dtype)

    def each(low, high, work):
        if a.reduce == b.reduce:

            def both(u):
                for side in sides:
                    work(side, u)

            loop(low, a.reduce + high, both)
        else:
            for side in sides:
                loop(low, side.reduce + high, functools.partial(work, side))

    each(0, 0, form)
    each(0, -1, lambda side, u: settle(side, u, True))
    for side in sides:
        settle(side, side.reduce - 1, False)

    @pl.when(tm < groups - 1)
    def _():
        for side in sides:
            for u in range(side.reduce):
                for off in range(side.slots):
                    end_copy(side, u, off).start()

    def send(side, u, g):
        for off in range(side.cores, side.slots):
            final_copy(side, u, off, g).start()
        for off in range(1, side.cores):
            final_copy(side, u, off, g).start()

    def send_last(g):
        for side in sides:
            send(side, side.reduce - 1, g)

    def send_rest(g):
        for side in sides:
            for u in range(side.reduce):
                send(side, u, g)

    loop(0, early, send_last)
    loop(early, pieces, send_rest)

    @pl.when(tm > 0)
    def _():
        for side in sides:
            for u in range(side.reduce):
                for off in range(side.slots):
                    end_copy(side, u, off).wait_recv()

    lane = lax.broadcasted_iota(jnp.int32, (16, half), 1)

    def transform(source, slot, r):
        parts = [source(s, slice(r * per, (r + 1) * per)).reshape(-1, lanes) for s in range(SETS)]
        x = jnp.concatenate(parts, axis=0)
        turned = jnp.concatenate([-x[:, half:], x[:, :half]], axis=1)
        both = jnp.concatenate([x, turned], axis=0)
        partial[slot, r] = jnp.dot(tab[r], both, preferred_element_type=jnp.float32)

    def on_rows(start, slot, store):
        values = []
        for r in range(radix):
            both = partial[slot, r, pl.ds(start, 16), :]
            values.append((both[:, :half], both[:, half:]))
        for q in range(radix):
            store(pl.ds(q * span + start, 16), combine(values, q))

    for r in range(radix):
        transform(lambda s, at: hv[s][:, at, :], 1, r)
    frame = lane % n_taps

    def keep_before(at, signal):
        for p in range(2):
            total = jnp.zeros((16, half), jnp.float32)
            for k in range(1, n_taps):
                back = n_taps - 1 - k
                moved = pltpu.roll(signal[p], (half - back) % half, 1) if back else signal[p]
                tap = jnp.broadcast_to(taps[k, at, :][:, half - 1 :], (16, half))
                total = total + jnp.where(frame < k, tap * moved, 0.0)
            before[at, p * half : (p + 1) * half] = total

    loop(0, span // 16, lambda n: on_rows(pl.multiple_of(n * 16, 16), 1, keep_before))

    def fetch_beam(n):
        return [
            pltpu.make_async_copy(spec[s].at[:, n], xin.at[n % 2, s], x_in.at[n % 2, s]) for s in range(SETS)
        ]

    def arrive(g):
        for side in sides:
            for u in range(side.reduce):
                for off in range(1, side.slots):
                    final_copy(side, u, off, g).wait_recv()

    def send_out(n):
        return pltpu.make_async_copy(oo.at[n % 2], out.at[n], o_out.at[n % 2])

    arrive(0)
    for copy in fetch_beam(0):
        copy.start()

    def synthesize(n):
        @pl.when(n < beams_local)
        def _():
            for copy in fetch_beam(n):
                copy.wait()

        more = jnp.logical_and((n + 1) % piece > 0, n + 1 < beams_local)

        @pl.when(more)
        def _():
            for copy in fetch_beam(n + 1):
                copy.start()

        @pl.when(n >= 3)
        def _():
            send_out(n - 3).wait()

        new, old = n % 2, (n + 1) % 2
        shift = (half - n_taps * jnp.maximum(n - 1, 0)) % half

        def store(at, signal):
            for p in range(2):
                cut = slice(p * half, (p + 1) * half)
                total = taps[0, at, :] * signal[p]
                for k in range(1, n_taps):
                    total = total + taps[k, at, :] * pltpu.roll(signal[p], k, 1)
                total = total + jnp.where(lane < tail, pltpu.roll(before[at, cut], shift, 1), 0.0)
                oo[old, at, cut] = total.astype(oo.dtype)

        for r in range(radix):
            transform(lambda s, at: xin[new, s, :, at, :], new, r)
            for start in range(r * span // radix, (r + 1) * span // radix, 16):
                on_rows(start, old, store)

        @pl.when(n >= 1)
        def _():
            send_out(n - 1).start()

        @pl.when(jnp.logical_and((n + 1) % piece == 0, n + 1 < beams_local))
        def _():
            arrive((n + 1) // piece)
            for copy in fetch_beam(n + 1):
                copy.start()

    loop(0, beams_local + 1, synthesize)
    for n in range(max(0, beams_local - 2), beams_local):
        send_out(n).wait()

    for side in sides:
        for off in range(1, side.slots):
            factor_copy(side, off).wait_send()
        for d in range(1, side.reduce):
            gain_copy(side, d).wait_send()

        def finish(u, side=side):
            for off in range(1, side.slots):
                raw_copy(side, u, off).wait_send()
                loop(0, pieces, lambda g: final_copy(side, u, off, g).wait_send())
            for d in range(1, side.reduce):
                part_copy(side, u, d).wait_send()

            @pl.when(tm < groups - 1)
            def _():
                for off in range(side.slots):
                    end_copy(side, u, off).wait_send()

        loop(0, side.reduce, finish)


def place_map(channels, devices, chunk_channels, radix):
    span = channels // radix
    per = chunk_channels // radix
    place = np.arange(span)
    chunk, source = place // (devices * per), place // per % devices
    channel = source * SETS * chunk_channels + chunk * chunk_channels + place % per * radix
    return jnp.asarray(np.broadcast_to(channel, (8, span)), jnp.int32)


def exchange(voltages, factors, gains, delays, filter_taps, grid, devices, beams, radix):
    per_station, channels, lanes = voltages.shape
    half = lanes // 2
    n_taps = filter_taps.shape[0]
    sides = [Side(s, grid) for s in range(SETS)]
    stations = factors[0].shape[1]
    beams_local = beams // devices
    local = channels // devices
    h = local // SETS
    span = channels // radix
    block = min(16, beams_local)
    piece = min(4, beams_local)
    most = max(side.slots for side in sides)
    deep = max(side.reduce for side in sides)
    bf, f32 = jnp.bfloat16, jnp.float32
    hbm = lambda *shape: jax.ShapeDtypeStruct(shape, bf)
    outs = [hbm(beams_local, channels, lanes)]
    outs += [hbm(devices, beams_local, h, lanes)] * 2
    outs += [hbm(side.reduce, side.slots, per_station, h, lanes) for side in sides]
    outs += [hbm(side.reduce, side.reduce, side.slots * beams_local, h, lanes) for side in sides] * 2
    outs += [hbm(side.reduce, side.slots, beams_local, h, lanes) for side in sides]
    any_space = pl.BlockSpec(memory_space=pl.ANY)
    vm = pltpu.VMEM
    blocks = factors[0].shape[0]
    base = place_map(channels, devices, h, radix)
    scratch = [
        vm((stations, h, lanes), bf),
        vm((stations * 16, half), f32),
        vm((stations * 16, half), f32),
        vm((QUAD, beams, stations), bf),
        vm((QUAD, beams, stations), bf),
        vm((beams, stations), f32),
        vm((beams, stations), f32),
        vm((beams * h, half), f32),
        vm((beams * h, half), f32),
        vm((2, block, h, lanes), bf),
        vm((radix, span, 2 * span), bf),
        vm((n_taps, channels, half), f32),
        vm((2, radix, span, lanes), f32),
        vm((channels, lanes), f32),
        vm((2, SETS, devices, h, lanes), bf),
        vm((2, channels, lanes), bf),
        vm(filter_taps.shape, f32),
        vm(base.shape, jnp.int32),
        vm((3, deep, block, h, lanes), bf),
        vm((2, block, h, lanes), bf),
    ]
    shares = lambda make: [make(side) for side in sides]
    scratch += shares(lambda side: vm((side.reduce, 2, side.group, side.cores * per_station, local), f32))
    scratch += shares(lambda side: vm((side.reduce, 2, h, stations), f32)) * 2
    scratch += shares(lambda side: vm((side.slots, blocks, stations), f32))
    scratch += shares(lambda side: vm((blocks, stations), f32))
    scratch += shares(lambda side: vm((side.group, side.cores * per_station, beams), f32))
    scratch += [vm((beams, stations), f32)] * 6
    scratch += shares(lambda side: vm((side.reduce, side.slots, h, lanes), f32))
    scratch += shares(lambda side: vm((side.reduce, side.slots, h, lanes), bf))
    scratch += shares(lambda side: vm((devices, h, lanes), bf))
    dma = pltpu.SemaphoreType.DMA
    scratch += [dma((SETS, deep, most))] * 2 + [dma((SETS, deep))] * 2 + [dma((SETS, most))] * 2
    scratch += [dma((SETS, deep, deep))] * 2 + [dma((SETS, deep, most, beams_local // piece))] * 2
    scratch += [dma((SETS, deep, most))] * 2
    scratch += [dma((SETS, deep, 2)), dma((SETS,)), dma((2,)), dma((SETS,)), dma((most,)), dma((2,))]
    scratch += [dma((3, deep)), dma((2,)), dma((2, SETS)), dma((2,))]
    results = pl.pallas_call(
        functools.partial(exchange_kernel, grid, n_taps, channels, radix),
        name="exchange",
        in_specs=[any_space] * 8,
        out_specs=[any_space] * len(outs),
        out_shape=outs,
        scratch_shapes=scratch,
        compiler_params=pltpu.CompilerParams(
            collective_id=0, has_side_effects=True, vmem_limit_bytes=VMEM_LIMIT
        ),
    )(voltages, *factors, *gains, delays, filter_taps, base)
    return results[0]


def times_unit(value, turn, radix):
    re, im = value
    quarter = turn * (4 // radix) % 4
    return ((re, im), (-im, re), (-re, -im), (im, -re))[quarter]


def combine(values, q):
    radix = len(values)
    re, im = values[0]
    for r in range(1, radix):
        more_re, more_im = times_unit(values[r], r * q, radix)
        re, im = re + more_re, im + more_im
    return re, im


def per_device(voltages, exponents, gain_real, gain_imag, delays, filter_taps):
    per_station, channels, lanes = voltages.shape
    devices = lax.axis_size("chan")
    local = channels // devices
    radix = radix_of(local // SETS)
    beams = delays.shape[1]
    grid = chip_grid(devices)
    rows, cols, cores = grid
    factor = jnp.exp2(exponents[:, :, 0].astype(jnp.float32)).astype(jnp.bfloat16).astype(jnp.float32)
    factors = []
    for s in range(SETS):
        side = Side(s, grid)
        e, r, k = side.place()
        here = lax.broadcasted_iota(jnp.int32, (1, side.slots, 1), 1) == e * cores + k
        placed = jnp.where(here, jnp.transpose(factor)[:, None, :], 0.0)
        factors.append(placed.reshape(factor.shape[1], side.slots * per_station))
    split = (rows, cols, cores * per_station)
    gains = [gain.reshape(*split, local) for gain in (gain_real, gain_imag)]
    return exchange(
        voltages, factors, gains, delays.reshape(*split, beams), filter_taps, grid, devices, beams, radix
    )


def solution(mesh):
    placed = (
        P("chan", None, "tm"),
        P("chan", None, "tm"),
        P(None, "chan"),
        P(None, "chan"),
        P(),
        P(),
    )
    return jax.shard_map(per_device, mesh=mesh, in_specs=placed, out_specs=P("chan", None, "tm"), check_vma=False)
```

```python
import functools
import math

import jax
import jax.numpy as jnp
from jax import lax
from jax.experimental import pallas as pl
from jax.experimental.pallas import tpu as pltpu
import numpy as np
from jax.sharding import PartitionSpec as P

TWO_PI = 6.283185307179586
SETS = 2
QUAD = 4
ODD = 1
VMEM_LIMIT = 60 * 1024 * 1024


def radix_of(chunk_channels):
    return max(r for r in (4, 2, 1) if chunk_channels % r == 0 and (chunk_channels // r) % 16 == 0 or r == 1)


def chip_grid(devices):
    cores = 2 if devices % 2 == 0 else 1
    chips = devices // cores
    rows = max(r for r in range(1, chips + 1) if chips % r == 0 and r * r <= chips)
    return rows, chips // rows, cores


class Side:
    def __init__(self, which, grid):
        self.rows, self.cols, self.cores = grid
        self.which = which
        self.group, self.reduce = (self.rows, self.cols) if which == 0 else (self.cols, self.rows)
        self.slots = self.group * self.cores

    def device(self, e, r, k):
        i, j = (e, r) if self.which == 0 else (r, e)
        return (i * self.cols + j) * self.cores + k

    def place(self):
        d = lax.axis_index("chan")
        k = d % self.cores
        j = d // self.cores % self.cols
        i = d // (self.cores * self.cols)
        return (i, j, k) if self.which == 0 else (j, i, k)

    def peer(self, off):
        e, r, k = self.place()
        e2 = (e + off // self.cores) % self.group
        k2 = (k + off % self.cores) % self.cores
        return e2 * self.cores + k2, self.device(e2, r, k2), e2, k2


def times_unit(value, turn, radix):
    re, im = value
    quarter = turn * (4 // radix) % 4
    return ((re, im), (-im, re), (-re, -im), (im, -re))[quarter]


def combine(values, q):
    radix = len(values)
    re, im = values[0]
    for r in range(1, radix):
        more_re, more_im = times_unit(values[r], r * q, radix)
        re, im = re + more_re, im + more_im
    return re, im


def transform(source, tab, partial, slot, r, per, half):
    parts = [source(s, slice(r * per, (r + 1) * per)).reshape(-1, 2 * half) for s in range(SETS)]
    x = jnp.concatenate(parts, axis=0)
    turned = jnp.concatenate([-x[:, half:], x[:, :half]], axis=1)
    both = jnp.concatenate([x, turned], axis=0)
    partial[slot, r] = jnp.dot(tab[r], both, preferred_element_type=jnp.float32)


def on_rows(partial, start, slot, store):
    radix, span, lanes = partial.shape[1:]
    half = lanes // 2
    values = []
    for r in range(radix):
        both = partial[slot, r, pl.ds(start, 16), :]
        values.append((both[:, :half], both[:, half:]))
    for q in range(radix):
        store(pl.ds(q * span + start, 16), combine(values, q))


def one_beam(n, behind, xin, tab, taps, partial, before, oo, begin=True, end=True):
    n_taps, _, half = taps.shape
    radix, span = partial.shape[1:3]
    per = xin.shape[3] // radix
    lane = lax.broadcasted_iota(jnp.int32, (16, half), 1)
    new, old = n % 2, (n + 1) % 2
    shift = (half - n_taps * behind) % half

    def store(at, signal):
        for p in range(2):
            cut = slice(p * half, (p + 1) * half)
            total = taps[0, at, :] * signal[p]
            for k in range(1, n_taps):
                total = total + taps[k, at, :] * pltpu.roll(signal[p], k, 1)
            total = total + jnp.where(lane < n_taps - 1, pltpu.roll(before[at, cut], shift, 1), 0.0)
            oo[old, at, cut] = total.astype(oo.dtype)

    for r in range(radix):
        if begin:
            transform(lambda s, at: xin[new, s, :, at, :], tab, partial, new, r, per, half)
        if end:
            for start in range(r * span // radix, (r + 1) * span // radix, 16):
                on_rows(partial, start, old, store)


def loop(low, high, work):
    def body(n, carry):
        work(n)
        return carry

    lax.fori_loop(low, high, body, 0)


def exchange_kernel(grid, n_taps, channels, radix, *refs):
    sides = [Side(s, grid) for s in range(SETS)]
    v, powers, gains, dl, ft, base = refs[0], refs[1], refs[2:4], refs[4], refs[5], refs[6]
    out, tab_out, taps_out, before_out = refs[7:11]
    spec, raw, part, got, done = (refs[11 + 2 * n : 13 + 2 * n] for n in range(5))
    scratch = refs[21:]
    xv, xf_re, xf_im, w_re, w_im, st_c, st_s, s_re, s_im, ob = scratch[:10]
    tab, taps, partial, before, xin, oo, ftv, basev = scratch[10:18]
    pa, pb = scratch[18:20]
    powers_in = scratch[20]
    pairs = (scratch[21 + 2 * n : 23 + 2 * n] for n in range(13))
    gt, gsel, gbuf, factors, fbuf, fsum, dtmp, dv, rot_c, rot_s, hal, hb, hv = pairs
    sems = scratch[47:]
    raw_s, raw_r, gain_s, gain_r, fac_s, fac_r, part_s, part_r, fin_s, fin_r, end_s, end_r = sems[:12]
    gain_in, delay_in, extra_in, load_in, out_sem, fetch_in, put_sem, x_in, o_out, keep_sem = sems[12:]

    per_station, _, lanes = v.shape
    half = lanes // 2
    beams_local = spec[0].shape[1]
    devices, h = spec[0].shape[0], spec[0].shape[2]
    beams = devices * beams_local
    local = channels // devices
    stations = st_c.shape[1]
    per = h // radix
    span = channels // radix
    tail = n_taps - 1
    groups = lax.axis_size("tm")
    tm = lax.axis_index("tm")
    block = ob.shape[1]
    lift, high = xf_re.shape[0] // stations, s_re.shape[0] // beams
    piece = beams_local // fin_s.shape[3]
    pieces = beams_local // piece
    ready = out.shape[0]
    early = max(1, 5 * pieces // 8)
    width = channels // fsum[0].shape[0]
    me = lax.axis_index("chan")
    rows, cols, cores = grid
    normalizer = 1.0 / math.sqrt(rows * cols * cores * per_station)

    bar = pltpu.get_barrier_semaphore()
    a, b = sides

    def greet(time, own):
        if own:
            pl.semaphore_signal(bar, inc=1, device_id={"tm": time, "chan": me})
        for off in range(1, a.slots):
            pl.semaphore_signal(bar, inc=1, device_id={"tm": time, "chan": a.peer(off)[1]})
        for off in range(b.cores, b.slots):
            pl.semaphore_signal(bar, inc=1, device_id={"tm": time, "chan": b.peer(off)[1]})

    friends = a.slots - 1 + b.slots - b.cores
    greet(tm, False)

    @pl.when(tm > 0)
    def _():
        greet(tm - 1, True)

    @pl.when(tm < groups - 1)
    def _():
        pl.semaphore_wait(bar, 2 * friends + 1)

    @pl.when(tm == groups - 1)
    def _():
        pl.semaphore_wait(bar, friends)

    def raw_copy(side, u, off):
        s = side.which
        e, r, k = side.place()
        _, device, e2, k2 = side.peer(off)
        start = pl.multiple_of(side.device(e2, u, k2) * local + s * h, h)
        return pltpu.make_async_remote_copy(
            v.at[:, pl.ds(start, h), :],
            raw[s].at[u, e * side.cores + k],
            raw_s.at[s, u, off],
            raw_r.at[s, u, off],
            device_id={"chan": device},
        )

    def gain_copy(side, d):
        s = side.which
        e, r, k = side.place()
        r2 = (r + d) % side.reduce
        return pltpu.make_async_remote_copy(
            gsel[s].at[r2],
            gbuf[s].at[r],
            gain_s.at[s, d],
            gain_r.at[s, d],
            device_id={"chan": side.device(e, r2, k)},
        )

    def factor_copy(side, off):
        s = side.which
        e, r, k = side.place()
        return pltpu.make_async_remote_copy(
            factors[s],
            fbuf[s].at[e * side.cores + k],
            fac_s.at[s, off],
            fac_r.at[s, off],
            device_id={"chan": side.peer(off)[1]},
        )

    def part_copy(side, u, d):
        s = side.which
        e, r, k = side.place()
        r2 = (r + d) % side.reduce
        return pltpu.make_async_remote_copy(
            part[s].at[u, r2],
            got[s].at[u, r],
            part_s.at[s, u, d],
            part_r.at[s, u, d],
            device_id={"chan": side.device(e, r2, k)},
        )

    def final_copy(side, u, off, g):
        s = side.which
        e, r, k = side.place()
        q, device, _, _ = side.peer(off)
        at = pl.ds(g * piece, piece)
        return pltpu.make_async_remote_copy(
            done[s].at[u, q, at],
            spec[s].at[side.device(e, u, k), at],
            fin_s.at[s, u, off, g],
            fin_r.at[s, u, off, g],
            device_id={"chan": device},
        )

    def end_copy(side, u, off):
        s = side.which
        e, r, k = side.place()
        q, device, _, _ = side.peer(off)
        return pltpu.make_async_remote_copy(
            hb[s].at[u, q],
            hv[s].at[side.device(e, u, k)],
            end_s.at[s, u, off],
            end_r.at[s, u, off],
            device_id={"tm": jnp.minimum(tm + 1, groups - 1), "chan": device},
        )

    def span_of(side, source, r):
        return source.at[:, r] if side.which == 0 else source.at[r]

    def start_raw(u):
        for side in sides:
            if u < side.reduce:
                for off in range(side.cores, side.slots):
                    raw_copy(side, u, off).start()
                for off in range(1, side.cores):
                    raw_copy(side, u, off).start()

    def aligned(n, size):
        return pl.ds(pl.multiple_of(n * size, size), size)

    start_raw(0)
    gain_loads, delay_loads = [], []
    for side in sides:
        s = side.which
        e, r, k = side.place()
        for r2 in range(side.reduce):
            for p in range(2):
                source = span_of(side, gains[p], r2)
                gain_loads.append(pltpu.make_async_copy(source, gt[s].at[r2, p], gain_in.at[s, r2, p]))
        delay_loads.append(pltpu.make_async_copy(span_of(side, dl, r), dtmp[s], delay_in.at[s]))
    extra = ((powers, powers_in), (ft, ftv), (base, basev))
    loads = [pltpu.make_async_copy(one, two, extra_in.at[n]) for n, (one, two) in enumerate(extra)]
    loads += gain_loads + delay_loads
    for load in loads:
        load.start()
    for load in loads:
        load.wait()
    power = jnp.exp2(powers_in[...].astype(jnp.float32)).astype(jnp.bfloat16).astype(jnp.float32)
    for side in sides:
        s = side.which
        e, r, k = side.place()
        mine = e * side.cores + k
        placed = jnp.transpose(jnp.concatenate([power] * side.slots, axis=0))
        place = lax.broadcasted_iota(jnp.int32, placed.shape, 1) // per_station
        factors[s][...] = jnp.where(place == mine, placed, 0.0)
        fbuf[s][mine] = factors[s][...]
        for r2 in range(side.reduce):
            for p in range(2):
                turned = jnp.transpose(gt[s][r2, p].reshape(stations, local))
                gsel[s][r2, p] = turned[s * h : (s + 1) * h] * normalizer
    for side in sides:
        s = side.which
        turned = jnp.transpose(dtmp[s][...].reshape(stations, beams))
        held = cores * beams_local
        for i in range(rows):
            for j in range(cols):
                e, r = (i, j) if s == 0 else (j, i)
                to = (r * side.group + e) * held
                at = (i * cols + j) * held
                dv[s][to : to + held, :] = turned[at : at + held]
    for side in sides:
        for off in range(1, side.slots):
            factor_copy(side, off).start()
        for d in range(1, side.reduce):
            gain_copy(side, d).start()
    for u in range(1, max(side.reduce for side in sides)):
        start_raw(u)

    for side in sides:
        s = side.which
        r = side.place()[1]
        gbuf[s][r] = gsel[s][r]

        def rotate(n, s=s):
            at = aligned(n, 16)
            angle = (TWO_PI / channels) * dv[s][at, :]
            rot_c[s][at, :] = jnp.cos(angle)
            rot_s[s][at, :] = jnp.sin(angle)

        loop(0, beams // 16, rotate)
    for r in range(radix):

        def tabulate(n, r=r):
            at = aligned(n, 16)
            sample = n * 16 + lax.broadcasted_iota(jnp.int32, (16, span), 0)
            product = sample * (basev[0:1, :] + r)
            product = product & (channels - 1) if channels & (channels - 1) == 0 else lax.rem(product, channels)
            phases = TWO_PI / channels * product.astype(jnp.float32)
            tab[r, at, :span] = (jnp.cos(phases) * (1.0 / math.sqrt(channels))).astype(tab.dtype)
            tab[r, at, span:] = (jnp.sin(phases) * (1.0 / math.sqrt(channels))).astype(tab.dtype)

        loop(0, span // 16, tabulate)

    def spread_taps(n):
        at = aligned(n, half)
        lane = lax.broadcasted_iota(jnp.int32, (half, half), 1)
        for k in range(n_taps):
            column = jnp.transpose(jnp.broadcast_to(ftv[k : k + 1, at], (half, half)))
            taps[k, at, :] = jnp.where(lane >= k, column, 0.0)

    loop(0, channels // half, spread_taps)
    for side in sides:
        s = side.which
        hal[s][...] = jnp.zeros_like(hal[s])
        for off in range(1, side.slots):
            factor_copy(side, off).wait_recv()
        for d in range(1, side.reduce):
            gain_copy(side, d).wait_recv()
        total = fbuf[s][0]
        for q in range(1, side.slots):
            total = total + fbuf[s][q]
        fsum[s][...] = total

    @pl.when(tm == 0)
    def _():
        for s in range(SETS):
            hv[s][...] = jnp.zeros_like(hv[s])

    def form(side, u):
        s = side.which
        e, r, k = side.place()
        first = side.device(e, u, k) * local + s * h
        loads = []
        for off in range(side.slots):
            q = side.peer(off)[0]
            if off == 0:
                source = v.at[:, pl.ds(pl.multiple_of(first, h), h), :]
            else:
                raw_copy(side, u, off).wait_recv()
                source = raw[s].at[u, q]
            loads.append(pltpu.make_async_copy(source, xv.at[pl.ds(q * per_station, per_station)], load_in.at[off]))
            loads[-1].start()

        turns = TWO_PI * ((first.astype(jnp.float32) + 0.5) / channels - 0.5)

        def begin(n):
            at = aligned(n, 16)
            angle = turns * dv[s][at, :]
            st_c[at, :] = jnp.cos(angle)
            st_s[at, :] = jnp.sin(angle)

        loop(0, beams // 16, begin)
        for load in loads:
            load.wait()

        def tile(t):
            def spread(n):
                x = xv[aligned(n, 16), aligned(t, 16), :].astype(jnp.float32)
                for i in range(16):
                    at = pl.ds((n * 16 + i) * lift, 16)
                    xf_re[at, :] = x[i, :, :half]
                    xf_im[at, :] = x[i, :, half:]

            loop(0, stations // 16, spread)

            def quad(g):
                c0 = t * 16 + g * QUAD
                pair = []
                for q in range(QUAD):
                    scale = fsum[s][pl.ds((first + c0 + q) // width, 1), :]
                    pair.append((gbuf[s][u, 0, pl.ds(c0 + q, 1), :] * scale, gbuf[s][u, 1, pl.ds(c0 + q, 1), :] * scale))

                def weigh(n):
                    at = aligned(n, 16)
                    c, d = st_c[at, :], st_s[at, :]
                    rc, rs = rot_c[s][at, :], rot_s[s][at, :]
                    for q in range(QUAD):
                        gr, gi = pair[q]
                        w_re[q, at, :] = (gr * c + gi * d).astype(jnp.bfloat16)
                        w_im[q, at, :] = (gi * c - gr * d).astype(jnp.bfloat16)
                        c, d = c * rc - d * rs, d * rc + c * rs
                    st_c[at, :], st_s[at, :] = c, d

                loop(0, beams // 16, weigh)
                for q in range(QUAD):
                    from_rows = pl.ds(g * QUAD + q, stations, stride=lift)
                    x = jnp.concatenate([xf_re[from_rows, :], xf_im[from_rows, :]], axis=1).astype(jnp.bfloat16)
                    real = jnp.dot(w_re[q], x, preferred_element_type=jnp.float32)
                    imag = jnp.dot(w_im[q], x, preferred_element_type=jnp.float32)
                    c = c0 + q
                    to_rows = pl.ds(c % radix * per + c // radix, beams, stride=high)
                    s_re[to_rows, :] = real[:, :half] - imag[:, half:]
                    s_im[to_rows, :] = real[:, half:] + imag[:, :half]

            loop(0, 16 // QUAD, quad)

        loop(0, h // 16, tile)

        held = side.slots * beams_local

        def put(n):
            to = part[s].at[u, n * block // held, pl.ds(n * block % held, block)]
            return pltpu.make_async_copy(ob.at[n % 2], to, out_sem.at[n % 2])

        def flush(n):
            @pl.when(n >= 2)
            def _():
                put(n - 2).wait()

            for i in range(block):
                at = pl.ds((n * block + i) * high, h)
                ob[n % 2, i, :, :half] = s_re[at, :].astype(ob.dtype)
                ob[n % 2, i, :, half:] = s_im[at, :].astype(ob.dtype)
            put(n).start()

        loop(0, beams // block, flush)
        for n in range(2):
            put(beams // block - 2 + n).wait()
        for d in range(1, side.reduce):
            part_copy(side, u, d).start()

    def settle(side, u, send):
        s = side.which
        e, r, k = side.place()
        slot = side.device(e, u, k)
        lane = lax.broadcasted_iota(jnp.int32, (h, half), 1)
        ahead = pa.shape[0] - 1
        count = beams_local // block * side.slots
        for d in range(1, side.reduce):
            part_copy(side, u, d).wait_recv()

        def where_of(n):
            return side.peer(n % side.slots)[0], n // side.slots

        def fetch(n):
            q, g = where_of(n)
            at = pl.ds(q * beams_local + g * block, block)
            now = n % (ahead + 1)
            copies = [pltpu.make_async_copy(part[s].at[u, r, at], pa.at[now, 0], fetch_in.at[now, 0])]
            for d in range(1, side.reduce):
                other = got[s].at[u, (r + d) % side.reduce, at]
                copies.append(pltpu.make_async_copy(other, pa.at[now, d], fetch_in.at[now, d]))
            return copies

        def put(n, own):
            q, g = where_of(n)
            at = pl.ds(g * block, block)
            to = spec[s].at[slot, at] if own else done[s].at[u, q, at]
            return pltpu.make_async_copy(pb.at[n % 2], to, put_sem.at[n % 2])

        def pass_on(n):
            put(n, False).wait()
            if send:
                for g in range(block // piece):
                    at = n // side.slots * (block // piece) + g

                    @pl.when(jnp.logical_and(n % side.slots > 0, at < early))
                    def _(at=at):
                        final_copy(side, u, n % side.slots, at).start()

        for n in range(min(ahead, count)):
            for copy in fetch(n):
                copy.start()

        def step(n):
            q, g = where_of(n)
            now = n % (ahead + 1)
            for copy in fetch(n):
                copy.wait()

            @pl.when(n + ahead < count)
            def _():
                for copy in fetch(n + ahead):
                    copy.start()

            def add(t):
                total = pa[now, 0, t].astype(jnp.float32)
                for d in range(1, side.reduce):
                    total = total + pa[now, d, t].astype(jnp.float32)
                pb[n % 2, t] = total.astype(pb.dtype)
                first = n_taps * (g * block + t)
                place = lane - first
                keep = jnp.logical_and(place >= 0, place < tail)
                for p in range(2):
                    at = slice(p * half, (p + 1) * half)
                    moved = pltpu.roll(total[:, at], (first + tail) % half, 1)
                    hal[s][u, q, :, at] = jnp.where(keep, moved, hal[s][u, q, :, at])

            def add_pair(t):
                add(2 * t)
                add(2 * t + 1)

            loop(0, block // 2, add_pair)

            @pl.when(n > 0)
            def _():
                pass_on(n - 1)

            @pl.when(n % side.slots == 0)
            def _():
                put(n, True).start()

            @pl.when(n % side.slots > 0)
            def _():
                put(n, False).start()

        loop(0, count, step)
        pass_on(count - 1)
        hb[s][u] = hal[s][u].astype(hb[s].dtype)

    def each(low, high, work):
        if a.reduce == b.reduce:

            def both(u):
                for side in sides:
                    work(side, u)

            loop(low, a.reduce + high, both)
        else:
            for side in sides:
                loop(low, side.reduce + high, functools.partial(work, side))

    each(0, 0, form)
    each(0, -1, lambda side, u: settle(side, u, True))
    for side in sides:
        settle(side, side.reduce - 1, False)

    @pl.when(tm < groups - 1)
    def _():
        for side in sides:
            for u in range(side.reduce):
                for off in range(side.slots):
                    end_copy(side, u, off).start()

    def send(side, u, g):
        for off in range(side.cores, side.slots):
            final_copy(side, u, off, g).start()
        for off in range(1, side.cores):
            final_copy(side, u, off, g).start()

    def send_last(g):
        for side in sides:
            send(side, side.reduce - 1, g)

    def send_rest(g):
        for side in sides:
            for u in range(side.reduce):
                send(side, u, g)

    loop(0, early, send_last)
    loop(early, pieces, send_rest)

    @pl.when(tm > 0)
    def _():
        for side in sides:
            for u in range(side.reduce):
                for off in range(side.slots):
                    end_copy(side, u, off).wait_recv()

    lane = lax.broadcasted_iota(jnp.int32, (16, half), 1)
    for r in range(radix):
        transform(lambda s, at: hv[s][:, at, :], tab, partial, 1, r, per, half)
    frame = lane % n_taps

    def keep_before(at, signal):
        for p in range(2):
            total = jnp.zeros((16, half), jnp.float32)
            for k in range(1, n_taps):
                back = n_taps - 1 - k
                moved = pltpu.roll(signal[p], (half - back) % half, 1) if back else signal[p]
                tap = jnp.broadcast_to(taps[k, at, :][:, half - 1 :], (16, half))
                total = total + jnp.where(frame < k, tap * moved, 0.0)
            before[at, p * half : (p + 1) * half] = total

    loop(0, span // 16, lambda n: on_rows(partial, pl.multiple_of(n * 16, 16), 1, keep_before))
    kept = [
        pltpu.make_async_copy(tab, tab_out, keep_sem.at[0]),
        pltpu.make_async_copy(taps, taps_out, keep_sem.at[1]),
        pltpu.make_async_copy(before, before_out, keep_sem.at[2]),
    ]
    for copy in kept:
        copy.start()

    def fetch_beam(n):
        return [
            pltpu.make_async_copy(spec[s].at[:, n], xin.at[n % 2, s], x_in.at[n % 2, s]) for s in range(SETS)
        ]

    def arrive(g):
        for side in sides:
            for u in range(side.reduce):
                for off in range(1, side.slots):
                    final_copy(side, u, off, g).wait_recv()

    def send_out(n):
        return pltpu.make_async_copy(oo.at[n % 2], out.at[n], o_out.at[n % 2])

    arrive(0)
    for copy in fetch_beam(0):
        copy.start()

    def synthesize(n):
        @pl.when(n < ready)
        def _():
            for copy in fetch_beam(n):
                copy.wait()

        more = jnp.logical_and((n + 1) % piece > 0, n + 1 < ready)

        @pl.when(more)
        def _():
            for copy in fetch_beam(n + 1):
                copy.start()

        @pl.when(n >= 3)
        def _():
            send_out(n - 3).wait()

        one_beam(n, jnp.maximum(n - 1, 0), xin, tab, taps, partial, before, oo)

        @pl.when(n >= 1)
        def _():
            send_out(n - 1).start()

        @pl.when(jnp.logical_and((n + 1) % piece == 0, n + 1 < ready))
        def _():
            arrive((n + 1) // piece)
            for copy in fetch_beam(n + 1):
                copy.start()

    loop(0, ready + 1, synthesize)
    arrive(pieces - 1)
    for n in range(max(0, ready - 2), ready):
        send_out(n).wait()
    for copy in kept:
        copy.wait()

    for side in sides:
        for off in range(1, side.slots):
            factor_copy(side, off).wait_send()
        for d in range(1, side.reduce):
            gain_copy(side, d).wait_send()

        def finish(u, side=side):
            for off in range(1, side.slots):
                raw_copy(side, u, off).wait_send()
                loop(0, pieces, lambda g: final_copy(side, u, off, g).wait_send())
            for d in range(1, side.reduce):
                part_copy(side, u, d).wait_send()

            @pl.when(tm < groups - 1)
            def _():
                for off in range(side.slots):
                    end_copy(side, u, off).wait_send()

        loop(0, side.reduce, finish)


def place_map(channels, devices, chunk_channels, radix):
    span = channels // radix
    per = chunk_channels // radix
    place = np.arange(span)
    chunk, source = place // (devices * per), place // per % devices
    channel = source * SETS * chunk_channels + chunk * chunk_channels + place % per * radix
    return jnp.asarray(np.broadcast_to(channel, (8, span)), jnp.int32)


def exchange(voltages, powers, gains, delays, filter_taps, grid, devices, beams, radix):
    per_station, channels, lanes = voltages.shape
    half = lanes // 2
    n_taps = filter_taps.shape[0]
    sides = [Side(s, grid) for s in range(SETS)]
    stations = max(side.slots for side in sides) * per_station
    beams_local = beams // devices
    local = channels // devices
    h = local // SETS
    span = channels // radix
    block = min(16, beams_local)
    piece = min(4, beams_local)
    most = max(side.slots for side in sides)
    deep = max(side.reduce for side in sides)
    bf, f32 = jnp.bfloat16, jnp.float32
    hbm = lambda *shape: jax.ShapeDtypeStruct(shape, bf)
    outs = [
        hbm(beams_local - piece, channels, lanes),
        hbm(radix, span, 2 * span),
        jax.ShapeDtypeStruct((n_taps, channels, half), f32),
        jax.ShapeDtypeStruct((channels, lanes), f32),
    ]
    outs += [hbm(devices, beams_local, h, lanes)] * 2
    outs += [hbm(side.reduce, side.slots, per_station, h, lanes) for side in sides]
    outs += [hbm(side.reduce, side.reduce, side.slots * beams_local, h, lanes) for side in sides] * 2
    outs += [hbm(side.reduce, side.slots, beams_local, h, lanes) for side in sides]
    any_space = pl.BlockSpec(memory_space=pl.ANY)
    vm = pltpu.VMEM
    blocks = powers.shape[1]
    base = place_map(channels, devices, h, radix)
    scratch = [
        vm((stations, h, lanes), bf),
        vm((stations * (16 + ODD), half), f32),
        vm((stations * (16 + ODD), half), f32),
        vm((QUAD, beams, stations), bf),
        vm((QUAD, beams, stations), bf),
        vm((beams, stations), f32),
        vm((beams, stations), f32),
        vm((beams * (h + ODD), half), f32),
        vm((beams * (h + ODD), half), f32),
        vm((2, block, h, lanes), bf),
        vm((radix, span, 2 * span), bf),
        vm((n_taps, channels, half), f32),
        vm((2, radix, span, lanes), f32),
        vm((channels, lanes), f32),
        vm((2, SETS, devices, h, lanes), bf),
        vm((2, channels, lanes), bf),
        vm(filter_taps.shape, f32),
        vm(base.shape, jnp.int32),
        vm((3, deep, block, h, lanes), bf),
        vm((2, block, h, lanes), bf),
        vm(powers.shape, jnp.int32),
    ]
    shares = lambda make: [make(side) for side in sides]
    scratch += shares(lambda side: vm((side.reduce, 2, side.group, side.cores * per_station, local), f32))
    scratch += shares(lambda side: vm((side.reduce, 2, h, stations), f32)) * 2
    scratch += shares(lambda side: vm((blocks, stations), f32))
    scratch += shares(lambda side: vm((side.slots, blocks, stations), f32))
    scratch += shares(lambda side: vm((blocks, stations), f32))
    scratch += shares(lambda side: vm((side.group, side.cores * per_station, beams), f32))
    scratch += [vm((beams, stations), f32)] * 6
    scratch += shares(lambda side: vm((side.reduce, side.slots, h, lanes), f32))
    scratch += shares(lambda side: vm((side.reduce, side.slots, h, lanes), bf))
    scratch += shares(lambda side: vm((devices, h, lanes), bf))
    dma = pltpu.SemaphoreType.DMA
    scratch += [dma((SETS, deep, most))] * 2 + [dma((SETS, deep))] * 2 + [dma((SETS, most))] * 2
    scratch += [dma((SETS, deep, deep))] * 2 + [dma((SETS, deep, most, beams_local // piece))] * 2
    scratch += [dma((SETS, deep, most))] * 2
    scratch += [dma((SETS, deep, 2)), dma((SETS,)), dma((3,)), dma((most,)), dma((2,))]
    scratch += [dma((3, deep)), dma((2,)), dma((2, SETS)), dma((2,)), dma((3,))]
    results = pl.pallas_call(
        functools.partial(exchange_kernel, grid, n_taps, channels, radix),
        name="exchange",
        in_specs=[any_space] * 7,
        out_specs=[any_space] * len(outs),
        out_shape=outs,
        scratch_shapes=scratch,
        compiler_params=pltpu.CompilerParams(
            collective_id=0, has_side_effects=True, vmem_limit_bytes=VMEM_LIMIT
        ),
    )(voltages, powers, *gains, delays, filter_taps, base)
    return conclude(*results[:6], beams_local)


def conclude_kernel(res, tab_in, taps_in, before_in, spec_a, spec_b, out, *scratch):
    tab, taps, before, xin, partial, oo, held, const_in, x_in, o_out, in_sem, out_sem = scratch
    spec = (spec_a, spec_b)
    first = res.shape[0]
    last = out.shape[0] - first
    size = held.shape[1]
    chunks = held.shape[0]

    def fetch_beam(n):
        return [pltpu.make_async_copy(spec[s].at[:, first + n], xin.at[n % 2, s], x_in.at[n % 2, s]) for s in range(SETS)]

    def send_out(n):
        return pltpu.make_async_copy(oo.at[n % 2], out.at[first + n], o_out.at[n % 2])

    consts = ((tab_in, tab), (taps_in, taps), (before_in, before))
    loads = [pltpu.make_async_copy(one, two, const_in.at[n]) for n, (one, two) in enumerate(consts)]
    takes = [pltpu.make_async_copy(res.at[pl.ds(c * size, size)], held.at[c], in_sem.at[c]) for c in range(chunks)]
    gives = [pltpu.make_async_copy(held.at[c], out.at[pl.ds(c * size, size)], out_sem.at[c]) for c in range(chunks)]
    for copy in fetch_beam(0) + loads + takes:
        copy.start()
    for copy in loads:
        copy.wait()
    moved = 0
    for n in range(last + 1):
        if n < last:
            for copy in fetch_beam(n):
                copy.wait()
        if n + 1 < last:
            for copy in fetch_beam(n + 1):
                copy.start()
        if n >= 3:
            send_out(n - 3).wait()
        one_beam(n, first + n - 1, xin, tab, taps, partial, before, oo, n < last, n > 0)
        if n >= 1:
            send_out(n - 1).start()
        upto = min(chunks, -(-chunks * (n + 1) // last))
        for c in range(moved, upto):
            takes[c].wait()
            gives[c].start()
        moved = max(moved, upto)
    for n in range(max(0, last - 2), last):
        send_out(n).wait()
    for copy in gives:
        copy.wait()


def conclude(res, tab, taps, before, spec_a, spec_b, beams_local):
    first, channels, lanes = res.shape
    devices, _, h, _ = spec_a.shape
    radix, span = tab.shape[:2]
    size = math.gcd(first, 4)
    vm, dma = pltpu.VMEM, pltpu.SemaphoreType.DMA
    any_space = pl.BlockSpec(memory_space=pl.ANY)
    return pl.pallas_call(
        conclude_kernel,
        name="conclude",
        in_specs=[any_space] * 6,
        out_specs=any_space,
        out_shape=jax.ShapeDtypeStruct((beams_local, channels, lanes), jnp.bfloat16),
        scratch_shapes=[
            vm(tab.shape, tab.dtype),
            vm(taps.shape, taps.dtype),
            vm(before.shape, before.dtype),
            vm((2, SETS, devices, h, lanes), jnp.bfloat16),
            vm((2, radix, span, lanes), jnp.float32),
            vm((2, channels, lanes), jnp.bfloat16),
            vm((first // size, size, channels, lanes), jnp.bfloat16),
            dma((3,)),
            dma((2, SETS)),
            dma((2,)),
            dma((first // size,)),
            dma((first // size,)),
        ],
        compiler_params=pltpu.CompilerParams(vmem_limit_bytes=VMEM_LIMIT),
    )(res, tab, taps, before, spec_a, spec_b)


def per_device(voltages, exponents, gain_real, gain_imag, delays, filter_taps):
    per_station, channels, lanes = voltages.shape
    devices = lax.axis_size("chan")
    local = channels // devices
    radix = radix_of(local // SETS)
    beams = delays.shape[1]
    grid = chip_grid(devices)
    rows, cols, cores = grid
    split = (rows, cols, cores * per_station)
    gains = [gain.reshape(*split, local) for gain in (gain_real, gain_imag)]
    return exchange(
        voltages, exponents[:, :, 0], gains, delays.reshape(*split, beams), filter_taps, grid, devices, beams, radix
    )


def solution(mesh):
    placed = (
        P("chan", None, "tm"),
        P("chan", None, "tm"),
        P(None, "chan"),
        P(None, "chan"),
        P(),
        P(),
    )
    return jax.shard_map(per_device, mesh=mesh, in_specs=placed, out_specs=P("chan", None, "tm"), check_vma=False)
```

```python
import functools
import math

import jax
import jax.numpy as jnp
from jax import lax
from jax.experimental import pallas as pl
from jax.experimental.pallas import tpu as pltpu
import numpy as np
from jax.sharding import PartitionSpec as P

TWO_PI = 6.283185307179586
SETS = 2
QUAD = 4
ODD = 1
VMEM_LIMIT = 60 * 1024 * 1024


def radix_of(chunk_channels):
    return max(r for r in (4, 2, 1) if chunk_channels % r == 0 and (chunk_channels // r) % 16 == 0 or r == 1)


def chip_grid(devices):
    cores = 2 if devices % 2 == 0 else 1
    chips = devices // cores
    rows = max(r for r in range(1, chips + 1) if chips % r == 0 and r * r <= chips)
    return rows, chips // rows, cores


class Side:
    def __init__(self, which, grid):
        self.rows, self.cols, self.cores = grid
        self.which = which
        self.group, self.reduce = (self.rows, self.cols) if which == 0 else (self.cols, self.rows)
        self.slots = self.group * self.cores

    def device(self, e, r, k):
        i, j = (e, r) if self.which == 0 else (r, e)
        return (i * self.cols + j) * self.cores + k

    def place(self):
        d = lax.axis_index("chan")
        k = d % self.cores
        j = d // self.cores % self.cols
        i = d // (self.cores * self.cols)
        return (i, j, k) if self.which == 0 else (j, i, k)

    def peer(self, off):
        e, r, k = self.place()
        e2 = (e + off // self.cores) % self.group
        k2 = (k + off % self.cores) % self.cores
        return e2 * self.cores + k2, self.device(e2, r, k2), e2, k2


def times_unit(value, turn, radix):
    re, im = value
    quarter = turn * (4 // radix) % 4
    return ((re, im), (-im, re), (-re, -im), (im, -re))[quarter]


def combine(values, q):
    radix = len(values)
    re, im = values[0]
    for r in range(1, radix):
        more_re, more_im = times_unit(values[r], r * q, radix)
        re, im = re + more_re, im + more_im
    return re, im


def transform(source, tab, partial, slot, r, per, half):
    parts = [source(s, slice(r * per, (r + 1) * per)).reshape(-1, 2 * half) for s in range(SETS)]
    x = jnp.concatenate(parts, axis=0)
    turned = jnp.concatenate([-x[:, half:], x[:, :half]], axis=1)
    both = jnp.concatenate([x, turned], axis=0)
    partial[slot, r] = jnp.dot(tab[r], both, preferred_element_type=jnp.float32)


def on_rows(partial, start, slot, store):
    radix, span, lanes = partial.shape[1:]
    half = lanes // 2
    values = []
    for r in range(radix):
        both = partial[slot, r, pl.ds(start, 16), :]
        values.append((both[:, :half], both[:, half:]))
    for q in range(radix):
        store(pl.ds(q * span + start, 16), combine(values, q))


def one_beam(n, behind, xin, tab, taps, partial, before, oo, begin=True, end=True):
    n_taps, _, half = taps.shape
    radix, span = partial.shape[1:3]
    per = xin.shape[3] // radix
    lane = lax.broadcasted_iota(jnp.int32, (16, half), 1)
    new, old = n % 2, (n + 1) % 2
    shift = (half - n_taps * behind) % half

    def store(at, signal):
        for p in range(2):
            cut = slice(p * half, (p + 1) * half)
            total = taps[0, at, :] * signal[p]
            for k in range(1, n_taps):
                total = total + taps[k, at, :] * pltpu.roll(signal[p], k, 1)
            total = total + jnp.where(lane < n_taps - 1, pltpu.roll(before[at, cut], shift, 1), 0.0)
            oo[old, at, cut] = total.astype(oo.dtype)

    for r in range(radix):
        if begin:
            transform(lambda s, at: xin[new, s, :, at, :], tab, partial, new, r, per, half)
        if end:
            for start in range(r * span // radix, (r + 1) * span // radix, 16):
                on_rows(partial, start, old, store)


def loop(low, high, work):
    def body(n, carry):
        work(n)
        return carry

    lax.fori_loop(low, high, body, 0)


def exchange_kernel(grid, n_taps, channels, radix, *refs):
    sides = [Side(s, grid) for s in range(SETS)]
    v, powers, gains, dl, ft, base = refs[0], refs[1], refs[2:4], refs[4], refs[5], refs[6]
    out, tab_out, taps_out, before_out = refs[7:11]
    spec, raw, part, got, done = (refs[11 + 2 * n : 13 + 2 * n] for n in range(5))
    scratch = refs[21:]
    xv, xf_re, xf_im, w_re, w_im, st_c, st_s, s_re, s_im, ob = scratch[:10]
    tab, taps, partial, before, xin, oo, ftv, basev = scratch[10:18]
    pa, pb = scratch[18:20]
    powers_in = scratch[20]
    pairs = (scratch[21 + 2 * n : 23 + 2 * n] for n in range(13))
    gt, gsel, gbuf, factors, fbuf, fsum, dtmp, dv, rot_c, rot_s, hal, hb, hv = pairs
    sems = scratch[47:]
    raw_s, raw_r, gain_s, gain_r, fac_s, fac_r, part_s, part_r, fin_s, fin_r, end_s, end_r = sems[:12]
    gain_in, delay_in, extra_in, load_in, out_sem, fetch_in, put_sem, x_in, o_out, keep_sem = sems[12:]

    per_station, _, lanes = v.shape
    half = lanes // 2
    beams_local = spec[0].shape[1]
    devices, h = spec[0].shape[0], spec[0].shape[2]
    beams = devices * beams_local
    local = channels // devices
    stations = st_c.shape[1]
    per = h // radix
    span = channels // radix
    tail = n_taps - 1
    groups = lax.axis_size("tm")
    tm = lax.axis_index("tm")
    block = ob.shape[1]
    lift, high = xf_re.shape[0] // stations, s_re.shape[0] // beams
    piece = beams_local // fin_s.shape[3]
    pieces = beams_local // piece
    ready = out.shape[0]
    early = max(1, 5 * pieces // 8)
    width = channels // fsum[0].shape[0]
    me = lax.axis_index("chan")
    rows, cols, cores = grid
    normalizer = 1.0 / math.sqrt(rows * cols * cores * per_station)

    bar = pltpu.get_barrier_semaphore()
    a, b = sides

    def greet(time, own):
        if own:
            pl.semaphore_signal(bar, inc=1, device_id={"tm": time, "chan": me})
        for off in range(1, a.slots):
            pl.semaphore_signal(bar, inc=1, device_id={"tm": time, "chan": a.peer(off)[1]})
        for off in range(b.cores, b.slots):
            pl.semaphore_signal(bar, inc=1, device_id={"tm": time, "chan": b.peer(off)[1]})

    friends = a.slots - 1 + b.slots - b.cores
    greet(tm, False)

    @pl.when(tm > 0)
    def _():
        greet(tm - 1, True)

    @pl.when(tm < groups - 1)
    def _():
        pl.semaphore_wait(bar, 2 * friends + 1)

    @pl.when(tm == groups - 1)
    def _():
        pl.semaphore_wait(bar, friends)

    def raw_copy(side, u, off):
        s = side.which
        e, r, k = side.place()
        _, device, e2, k2 = side.peer(off)
        start = pl.multiple_of(side.device(e2, u, k2) * local + s * h, h)
        return pltpu.make_async_remote_copy(
            v.at[:, pl.ds(start, h), :],
            raw[s].at[u, e * side.cores + k],
            raw_s.at[s, u, off],
            raw_r.at[s, u, off],
            device_id={"chan": device},
        )

    def gain_copy(side, d):
        s = side.which
        e, r, k = side.place()
        r2 = (r + d) % side.reduce
        return pltpu.make_async_remote_copy(
            gsel[s].at[r2],
            gbuf[s].at[r],
            gain_s.at[s, d],
            gain_r.at[s, d],
            device_id={"chan": side.device(e, r2, k)},
        )

    def factor_copy(side, off):
        s = side.which
        e, r, k = side.place()
        return pltpu.make_async_remote_copy(
            factors[s],
            fbuf[s].at[e * side.cores + k],
            fac_s.at[s, off],
            fac_r.at[s, off],
            device_id={"chan": side.peer(off)[1]},
        )

    def part_copy(side, u, d):
        s = side.which
        e, r, k = side.place()
        r2 = (r + d) % side.reduce
        return pltpu.make_async_remote_copy(
            part[s].at[u, r2],
            got[s].at[u, r],
            part_s.at[s, u, d],
            part_r.at[s, u, d],
            device_id={"chan": side.device(e, r2, k)},
        )

    def final_copy(side, u, off, g):
        s = side.which
        e, r, k = side.place()
        q, device, _, _ = side.peer(off)
        at = pl.ds(g * piece, piece)
        return pltpu.make_async_remote_copy(
            done[s].at[u, q, at],
            spec[s].at[side.device(e, u, k), at],
            fin_s.at[s, u, off, g],
            fin_r.at[s, u, off, g],
            device_id={"chan": device},
        )

    def end_copy(side, u, off):
        s = side.which
        e, r, k = side.place()
        q, device, _, _ = side.peer(off)
        return pltpu.make_async_remote_copy(
            hb[s].at[u, q],
            hv[s].at[side.device(e, u, k)],
            end_s.at[s, u, off],
            end_r.at[s, u, off],
            device_id={"tm": jnp.minimum(tm + 1, groups - 1), "chan": device},
        )

    def span_of(side, source, r):
        return source.at[:, r] if side.which == 0 else source.at[r]

    def start_raw(u):
        for side in sides:
            if u < side.reduce:
                for off in range(side.cores, side.slots):
                    raw_copy(side, u, off).start()
                for off in range(1, side.cores):
                    raw_copy(side, u, off).start()

    def aligned(n, size):
        return pl.ds(pl.multiple_of(n * size, size), size)

    start_raw(0)
    gain_loads, delay_loads = [], []
    for side in sides:
        s = side.which
        e, r, k = side.place()
        for r2 in range(side.reduce):
            for p in range(2):
                source = span_of(side, gains[p], r2)
                gain_loads.append(pltpu.make_async_copy(source, gt[s].at[r2, p], gain_in.at[s, r2, p]))
        delay_loads.append(pltpu.make_async_copy(span_of(side, dl, r), dtmp[s], delay_in.at[s]))
    extra = ((powers, powers_in), (ft, ftv), (base, basev))
    loads = [pltpu.make_async_copy(one, two, extra_in.at[n]) for n, (one, two) in enumerate(extra)]
    loads += gain_loads + delay_loads
    for load in loads:
        load.start()
    for load in loads:
        load.wait()
    power = jnp.exp2(powers_in[...].astype(jnp.float32)).astype(jnp.bfloat16).astype(jnp.float32)
    for side in sides:
        s = side.which
        e, r, k = side.place()
        mine = e * side.cores + k
        place = lax.broadcasted_iota(jnp.int32, (1, stations), 1) // per_station
        for n in range(powers.shape[0]):
            placed = jnp.concatenate([power[n]] * side.slots, axis=1)
            factors[s][n : n + 1, :] = jnp.where(place == mine, placed, 0.0)
        fbuf[s][mine] = factors[s][...]
        for r2 in range(side.reduce):
            for p in range(2):
                turned = jnp.transpose(gt[s][r2, p].reshape(stations, local))
                gsel[s][r2, p] = turned[s * h : (s + 1) * h] * normalizer
    for side in sides:
        s = side.which
        turned = jnp.transpose(dtmp[s][...].reshape(stations, beams))
        held = cores * beams_local
        for i in range(rows):
            for j in range(cols):
                e, r = (i, j) if s == 0 else (j, i)
                to = (r * side.group + e) * held
                at = (i * cols + j) * held
                dv[s][to : to + held, :] = turned[at : at + held]
    for side in sides:
        for off in range(1, side.slots):
            factor_copy(side, off).start()
        for d in range(1, side.reduce):
            gain_copy(side, d).start()
    for u in range(1, max(side.reduce for side in sides)):
        start_raw(u)

    for side in sides:
        s = side.which
        r = side.place()[1]
        gbuf[s][r] = gsel[s][r]

        def rotate(n, s=s):
            at = aligned(n, 16)
            angle = (TWO_PI / channels) * dv[s][at, :]
            rot_c[s][at, :] = jnp.cos(angle)
            rot_s[s][at, :] = jnp.sin(angle)

        loop(0, beams // 16, rotate)
    for r in range(radix):

        def tabulate(n, r=r):
            at = aligned(n, 16)
            sample = n * 16 + lax.broadcasted_iota(jnp.int32, (16, span), 0)
            product = sample * (basev[0:1, :] + r)
            product = product & (channels - 1) if channels & (channels - 1) == 0 else lax.rem(product, channels)
            phases = TWO_PI / channels * product.astype(jnp.float32)
            tab[r, at, :span] = (jnp.cos(phases) * (1.0 / math.sqrt(channels))).astype(tab.dtype)
            tab[r, at, span:] = (jnp.sin(phases) * (1.0 / math.sqrt(channels))).astype(tab.dtype)

        loop(0, span // 16, tabulate)

    def spread_taps(n):
        at = aligned(n, half)
        lane = lax.broadcasted_iota(jnp.int32, (half, half), 1)
        for k in range(n_taps):
            column = jnp.transpose(jnp.broadcast_to(ftv[k : k + 1, at], (half, half)))
            taps[k, at, :] = jnp.where(lane >= k, column, 0.0)

    loop(0, channels // half, spread_taps)
    for side in sides:
        s = side.which
        hal[s][...] = jnp.zeros_like(hal[s])
        for off in range(1, side.slots):
            factor_copy(side, off).wait_recv()
        for d in range(1, side.reduce):
            gain_copy(side, d).wait_recv()
        total = fbuf[s][0]
        for q in range(1, side.slots):
            total = total + fbuf[s][q]
        fsum[s][...] = total

    @pl.when(tm == 0)
    def _():
        for s in range(SETS):
            hv[s][...] = jnp.zeros_like(hv[s])

    def form(side, u):
        s = side.which
        e, r, k = side.place()
        first = side.device(e, u, k) * local + s * h
        loads = []
        for off in range(side.slots):
            q = side.peer(off)[0]
            if off == 0:
                source = v.at[:, pl.ds(pl.multiple_of(first, h), h), :]
            else:
                raw_copy(side, u, off).wait_recv()
                source = raw[s].at[u, q]
            loads.append(pltpu.make_async_copy(source, xv.at[pl.ds(q * per_station, per_station)], load_in.at[off]))
            loads[-1].start()

        turns = TWO_PI * ((first.astype(jnp.float32) + 0.5) / channels - 0.5)

        def begin(n):
            at = aligned(n, 16)
            angle = turns * dv[s][at, :]
            st_c[at, :] = jnp.cos(angle)
            st_s[at, :] = jnp.sin(angle)

        loop(0, beams // 16, begin)
        for load in loads:
            load.wait()

        def tile(t):
            def spread(n):
                x = xv[aligned(n, 16), aligned(t, 16), :].astype(jnp.float32)
                for i in range(16):
                    at = pl.ds((n * 16 + i) * lift, 16)
                    xf_re[at, :] = x[i, :, :half]
                    xf_im[at, :] = x[i, :, half:]

            loop(0, stations // 16, spread)

            def quad(g):
                c0 = t * 16 + g * QUAD
                pair = []
                for q in range(QUAD):
                    scale = fsum[s][pl.ds((first + c0 + q) // width, 1), :]
                    pair.append((gbuf[s][u, 0, pl.ds(c0 + q, 1), :] * scale, gbuf[s][u, 1, pl.ds(c0 + q, 1), :] * scale))

                def weigh(n):
                    at = aligned(n, 16)
                    c, d = st_c[at, :], st_s[at, :]
                    rc, rs = rot_c[s][at, :], rot_s[s][at, :]
                    for q in range(QUAD):
                        gr, gi = pair[q]
                        w_re[q, at, :] = (gr * c + gi * d).astype(jnp.bfloat16)
                        w_im[q, at, :] = (gi * c - gr * d).astype(jnp.bfloat16)
                        c, d = c * rc - d * rs, d * rc + c * rs
                    st_c[at, :], st_s[at, :] = c, d

                loop(0, beams // 16, weigh)
                for q in range(QUAD):
                    from_rows = pl.ds(g * QUAD + q, stations, stride=lift)
                    x = jnp.concatenate([xf_re[from_rows, :], xf_im[from_rows, :]], axis=1).astype(jnp.bfloat16)
                    real = jnp.dot(w_re[q], x, preferred_element_type=jnp.float32)
                    imag = jnp.dot(w_im[q], x, preferred_element_type=jnp.float32)
                    c = c0 + q
                    to_rows = pl.ds(c % radix * per + c // radix, beams, stride=high)
                    s_re[to_rows, :] = real[:, :half] - imag[:, half:]
                    s_im[to_rows, :] = real[:, half:] + imag[:, :half]

            loop(0, 16 // QUAD, quad)

        loop(0, h // 16, tile)

        held = side.slots * beams_local

        def put(n):
            to = part[s].at[u, n * block // held, pl.ds(n * block % held, block)]
            return pltpu.make_async_copy(ob.at[n % 2], to, out_sem.at[n % 2])

        def flush(n):
            @pl.when(n >= 2)
            def _():
                put(n - 2).wait()

            for i in range(block):
                at = pl.ds((n * block + i) * high, h)
                ob[n % 2, i, :, :half] = s_re[at, :].astype(ob.dtype)
                ob[n % 2, i, :, half:] = s_im[at, :].astype(ob.dtype)
            put(n).start()

        loop(0, beams // block, flush)
        for n in range(2):
            put(beams // block - 2 + n).wait()
        for d in range(1, side.reduce):
            part_copy(side, u, d).start()

    def settle(side, u, send):
        s = side.which
        e, r, k = side.place()
        slot = side.device(e, u, k)
        lane = lax.broadcasted_iota(jnp.int32, (h, half), 1)
        ahead = pa.shape[0] - 1
        count = beams_local // block * side.slots
        for d in range(1, side.reduce):
            part_copy(side, u, d).wait_recv()

        def where_of(n):
            return side.peer(n % side.slots)[0], n // side.slots

        def fetch(n):
            q, g = where_of(n)
            at = pl.ds(q * beams_local + g * block, block)
            now = n % (ahead + 1)
            copies = [pltpu.make_async_copy(part[s].at[u, r, at], pa.at[now, 0], fetch_in.at[now, 0])]
            for d in range(1, side.reduce):
                other = got[s].at[u, (r + d) % side.reduce, at]
                copies.append(pltpu.make_async_copy(other, pa.at[now, d], fetch_in.at[now, d]))
            return copies

        def put(n, own):
            q, g = where_of(n)
            at = pl.ds(g * block, block)
            to = spec[s].at[slot, at] if own else done[s].at[u, q, at]
            return pltpu.make_async_copy(pb.at[n % 2], to, put_sem.at[n % 2])

        def pass_on(n):
            put(n, False).wait()
            if send:
                for g in range(block // piece):
                    at = n // side.slots * (block // piece) + g

                    @pl.when(jnp.logical_and(n % side.slots > 0, at < early))
                    def _(at=at):
                        final_copy(side, u, n % side.slots, at).start()

        for n in range(min(ahead, count)):
            for copy in fetch(n):
                copy.start()

        def step(n):
            q, g = where_of(n)
            now = n % (ahead + 1)
            for copy in fetch(n):
                copy.wait()

            @pl.when(n + ahead < count)
            def _():
                for copy in fetch(n + ahead):
                    copy.start()

            def add(t):
                total = pa[now, 0, t].astype(jnp.float32)
                for d in range(1, side.reduce):
                    total = total + pa[now, d, t].astype(jnp.float32)
                pb[n % 2, t] = total.astype(pb.dtype)
                first = n_taps * (g * block + t)
                place = lane - first
                keep = jnp.logical_and(place >= 0, place < tail)
                for p in range(2):
                    at = slice(p * half, (p + 1) * half)
                    moved = pltpu.roll(total[:, at], (first + tail) % half, 1)
                    hal[s][u, q, :, at] = jnp.where(keep, moved, hal[s][u, q, :, at])

            def add_pair(t):
                add(2 * t)
                add(2 * t + 1)

            loop(0, block // 2, add_pair)

            @pl.when(n > 0)
            def _():
                pass_on(n - 1)

            @pl.when(n % side.slots == 0)
            def _():
                put(n, True).start()

            @pl.when(n % side.slots > 0)
            def _():
                put(n, False).start()

        loop(0, count, step)
        pass_on(count - 1)
        hb[s][u] = hal[s][u].astype(hb[s].dtype)

    def each(low, high, work):
        if a.reduce == b.reduce:

            def both(u):
                for side in sides:
                    work(side, u)

            loop(low, a.reduce + high, both)
        else:
            for side in sides:
                loop(low, side.reduce + high, functools.partial(work, side))

    each(0, 0, form)
    each(0, -1, lambda side, u: settle(side, u, True))
    for side in sides:
        settle(side, side.reduce - 1, False)

    @pl.when(tm < groups - 1)
    def _():
        for side in sides:
            for u in range(side.reduce):
                for off in range(side.slots):
                    end_copy(side, u, off).start()

    def send(side, u, g):
        for off in range(side.cores, side.slots):
            final_copy(side, u, off, g).start()
        for off in range(1, side.cores):
            final_copy(side, u, off, g).start()

    def send_last(g):
        for side in sides:
            send(side, side.reduce - 1, g)

    def send_rest(g):
        for side in sides:
            for u in range(side.reduce):
                send(side, u, g)

    loop(0, early, send_last)
    loop(early, pieces, send_rest)

    @pl.when(tm > 0)
    def _():
        for side in sides:
            for u in range(side.reduce):
                for off in range(side.slots):
                    end_copy(side, u, off).wait_recv()

    lane = lax.broadcasted_iota(jnp.int32, (16, half), 1)
    for r in range(radix):
        transform(lambda s, at: hv[s][:, at, :], tab, partial, 1, r, per, half)
    frame = lane % n_taps

    def keep_before(at, signal):
        for p in range(2):
            total = jnp.zeros((16, half), jnp.float32)
            for k in range(1, n_taps):
                back = n_taps - 1 - k
                moved = pltpu.roll(signal[p], (half - back) % half, 1) if back else signal[p]
                tap = jnp.broadcast_to(taps[k, at, :][:, half - 1 :], (16, half))
                total = total + jnp.where(frame < k, tap * moved, 0.0)
            before[at, p * half : (p + 1) * half] = total

    loop(0, span // 16, lambda n: on_rows(partial, pl.multiple_of(n * 16, 16), 1, keep_before))
    kept = [
        pltpu.make_async_copy(tab, tab_out, keep_sem.at[0]),
        pltpu.make_async_copy(taps, taps_out, keep_sem.at[1]),
        pltpu.make_async_copy(before, before_out, keep_sem.at[2]),
    ]
    for copy in kept:
        copy.start()

    def fetch_beam(n):
        return [
            pltpu.make_async_copy(spec[s].at[:, n], xin.at[n % 2, s], x_in.at[n % 2, s]) for s in range(SETS)
        ]

    def arrive(g):
        for side in sides:
            for u in range(side.reduce):
                for off in range(1, side.slots):
                    final_copy(side, u, off, g).wait_recv()

    def send_out(n):
        return pltpu.make_async_copy(oo.at[n % 2], out.at[n], o_out.at[n % 2])

    arrive(0)
    for copy in fetch_beam(0):
        copy.start()

    def synthesize(n):
        @pl.when(n < ready)
        def _():
            for copy in fetch_beam(n):
                copy.wait()

        @pl.when(n + 1 < ready)
        def _():
            @pl.when((n + 1) % piece == 0)
            def _():
                arrive((n + 1) // piece)

            for copy in fetch_beam(n + 1):
                copy.start()

        @pl.when(n >= 3)
        def _():
            send_out(n - 3).wait()

        one_beam(n, jnp.maximum(n - 1, 0), xin, tab, taps, partial, before, oo)

        @pl.when(n >= 1)
        def _():
            send_out(n - 1).start()

    loop(0, ready + 1, synthesize)
    arrive(pieces - 1)
    for n in range(max(0, ready - 2), ready):
        send_out(n).wait()
    for copy in kept:
        copy.wait()

    for side in sides:
        for off in range(1, side.slots):
            factor_copy(side, off).wait_send()
        for d in range(1, side.reduce):
            gain_copy(side, d).wait_send()

        def finish(u, side=side):
            for off in range(1, side.slots):
                raw_copy(side, u, off).wait_send()
                loop(0, pieces, lambda g: final_copy(side, u, off, g).wait_send())
            for d in range(1, side.reduce):
                part_copy(side, u, d).wait_send()

            @pl.when(tm < groups - 1)
            def _():
                for off in range(side.slots):
                    end_copy(side, u, off).wait_send()

        loop(0, side.reduce, finish)


def place_map(channels, devices, chunk_channels, radix):
    span = channels // radix
    per = chunk_channels // radix
    place = np.arange(span)
    chunk, source = place // (devices * per), place // per % devices
    channel = source * SETS * chunk_channels + chunk * chunk_channels + place % per * radix
    return jnp.asarray(np.broadcast_to(channel, (8, span)), jnp.int32)


def exchange(voltages, powers, gains, delays, filter_taps, grid, devices, beams, radix):
    per_station, channels, lanes = voltages.shape
    half = lanes // 2
    n_taps = filter_taps.shape[0]
    sides = [Side(s, grid) for s in range(SETS)]
    stations = max(side.slots for side in sides) * per_station
    beams_local = beams // devices
    local = channels // devices
    h = local // SETS
    span = channels // radix
    block = min(16, beams_local)
    piece = min(4, beams_local)
    most = max(side.slots for side in sides)
    deep = max(side.reduce for side in sides)
    bf, f32 = jnp.bfloat16, jnp.float32
    hbm = lambda *shape: jax.ShapeDtypeStruct(shape, bf)
    outs = [
        hbm(beams_local - piece, channels, lanes),
        hbm(radix, span, 2 * span),
        jax.ShapeDtypeStruct((n_taps, channels, half), f32),
        jax.ShapeDtypeStruct((channels, lanes), f32),
    ]
    outs += [hbm(devices, beams_local, h, lanes)] * 2
    outs += [hbm(side.reduce, side.slots, per_station, h, lanes) for side in sides]
    outs += [hbm(side.reduce, side.reduce, side.slots * beams_local, h, lanes) for side in sides] * 2
    outs += [hbm(side.reduce, side.slots, beams_local, h, lanes) for side in sides]
    any_space = pl.BlockSpec(memory_space=pl.ANY)
    vm = pltpu.VMEM
    blocks = powers.shape[0]
    base = place_map(channels, devices, h, radix)
    scratch = [
        vm((stations, h, lanes), bf),
        vm((stations * (16 + ODD), half), f32),
        vm((stations * (16 + ODD), half), f32),
        vm((QUAD, beams, stations), bf),
        vm((QUAD, beams, stations), bf),
        vm((beams, stations), f32),
        vm((beams, stations), f32),
        vm((beams * (h + ODD), half), f32),
        vm((beams * (h + ODD), half), f32),
        vm((2, block, h, lanes), bf),
        vm((radix, span, 2 * span), bf),
        vm((n_taps, channels, half), f32),
        vm((2, radix, span, lanes), f32),
        vm((channels, lanes), f32),
        vm((2, SETS, devices, h, lanes), bf),
        vm((2, channels, lanes), bf),
        vm(filter_taps.shape, f32),
        vm(base.shape, jnp.int32),
        vm((3, deep, block, h, lanes), bf),
        vm((2, block, h, lanes), bf),
        vm(powers.shape, jnp.int32),
    ]
    shares = lambda make: [make(side) for side in sides]
    scratch += shares(lambda side: vm((side.reduce, 2, side.group, side.cores * per_station, local), f32))
    scratch += shares(lambda side: vm((side.reduce, 2, h, stations), f32)) * 2
    scratch += shares(lambda side: vm((blocks, stations), f32))
    scratch += shares(lambda side: vm((side.slots, blocks, stations), f32))
    scratch += shares(lambda side: vm((blocks, stations), f32))
    scratch += shares(lambda side: vm((side.group, side.cores * per_station, beams), f32))
    scratch += [vm((beams, stations), f32)] * 6
    scratch += shares(lambda side: vm((side.reduce, side.slots, h, lanes), f32))
    scratch += shares(lambda side: vm((side.reduce, side.slots, h, lanes), bf))
    scratch += shares(lambda side: vm((devices, h, lanes), bf))
    dma = pltpu.SemaphoreType.DMA
    scratch += [dma((SETS, deep, most))] * 2 + [dma((SETS, deep))] * 2 + [dma((SETS, most))] * 2
    scratch += [dma((SETS, deep, deep))] * 2 + [dma((SETS, deep, most, beams_local // piece))] * 2
    scratch += [dma((SETS, deep, most))] * 2
    scratch += [dma((SETS, deep, 2)), dma((SETS,)), dma((3,)), dma((most,)), dma((2,))]
    scratch += [dma((3, deep)), dma((2,)), dma((2, SETS)), dma((2,)), dma((3,))]
    results = pl.pallas_call(
        functools.partial(exchange_kernel, grid, n_taps, channels, radix),
        name="exchange",
        in_specs=[any_space] * 7,
        out_specs=[any_space] * len(outs),
        out_shape=outs,
        scratch_shapes=scratch,
        compiler_params=pltpu.CompilerParams(
            collective_id=0, has_side_effects=True, vmem_limit_bytes=VMEM_LIMIT
        ),
    )(voltages, powers, *gains, delays, filter_taps, base)
    return conclude(*results[:6], beams_local)


def conclude_kernel(res, tab_in, taps_in, before_in, spec_a, spec_b, out, *scratch):
    tab, taps, before, xin, partial, oo, held, const_in, x_in, o_out, in_sem, out_sem = scratch
    spec = (spec_a, spec_b)
    first = res.shape[0]
    last = out.shape[0] - first
    size = held.shape[1]
    chunks = held.shape[0]

    def fetch_beam(n):
        return [pltpu.make_async_copy(spec[s].at[:, first + n], xin.at[n % 2, s], x_in.at[n % 2, s]) for s in range(SETS)]

    def send_out(n):
        return pltpu.make_async_copy(oo.at[n % 2], out.at[first + n], o_out.at[n % 2])

    consts = ((tab_in, tab), (taps_in, taps), (before_in, before))
    loads = [pltpu.make_async_copy(one, two, const_in.at[n]) for n, (one, two) in enumerate(consts)]
    takes = [pltpu.make_async_copy(res.at[pl.ds(c * size, size)], held.at[c], in_sem.at[c]) for c in range(chunks)]
    gives = [pltpu.make_async_copy(held.at[c], out.at[pl.ds(c * size, size)], out_sem.at[c]) for c in range(chunks)]
    for copy in fetch_beam(0) + loads + takes:
        copy.start()
    for copy in loads:
        copy.wait()
    moved = 0
    for n in range(last + 1):
        if n < last:
            for copy in fetch_beam(n):
                copy.wait()
        if n + 1 < last:
            for copy in fetch_beam(n + 1):
                copy.start()
        if n >= 3:
            send_out(n - 3).wait()
        one_beam(n, first + n - 1, xin, tab, taps, partial, before, oo, n < last, n > 0)
        if n >= 1:
            send_out(n - 1).start()
        upto = min(chunks, -(-chunks * (n + 1) // last))
        for c in range(moved, upto):
            takes[c].wait()
            gives[c].start()
        moved = max(moved, upto)
    for n in range(max(0, last - 2), last):
        send_out(n).wait()
    for copy in gives:
        copy.wait()


def conclude(res, tab, taps, before, spec_a, spec_b, beams_local):
    first, channels, lanes = res.shape
    devices, _, h, _ = spec_a.shape
    radix, span = tab.shape[:2]
    size = math.gcd(first, 4)
    vm, dma = pltpu.VMEM, pltpu.SemaphoreType.DMA
    any_space = pl.BlockSpec(memory_space=pl.ANY)
    return pl.pallas_call(
        conclude_kernel,
        name="conclude",
        in_specs=[any_space] * 6,
        out_specs=any_space,
        out_shape=jax.ShapeDtypeStruct((beams_local, channels, lanes), jnp.bfloat16),
        scratch_shapes=[
            vm(tab.shape, tab.dtype),
            vm(taps.shape, taps.dtype),
            vm(before.shape, before.dtype),
            vm((2, SETS, devices, h, lanes), jnp.bfloat16),
            vm((2, radix, span, lanes), jnp.float32),
            vm((2, channels, lanes), jnp.bfloat16),
            vm((first // size, size, channels, lanes), jnp.bfloat16),
            dma((3,)),
            dma((2, SETS)),
            dma((2,)),
            dma((first // size,)),
            dma((first // size,)),
        ],
        compiler_params=pltpu.CompilerParams(vmem_limit_bytes=VMEM_LIMIT),
    )(res, tab, taps, before, spec_a, spec_b)


def per_device(voltages, exponents, gain_real, gain_imag, delays, filter_taps):
    per_station, channels, lanes = voltages.shape
    devices = lax.axis_size("chan")
    local = channels // devices
    radix = radix_of(local // SETS)
    beams = delays.shape[1]
    grid = chip_grid(devices)
    rows, cols, cores = grid
    split = (rows, cols, cores * per_station)
    gains = [gain.reshape(*split, local) for gain in (gain_real, gain_imag)]
    return exchange(
        voltages, jnp.transpose(exponents, (1, 2, 0)), gains, delays.reshape(*split, beams), filter_taps, grid, devices, beams, radix
    )


def solution(mesh):
    placed = (
        P("chan", None, "tm"),
        P("chan", None, "tm"),
        P(None, "chan"),
        P(None, "chan"),
        P(),
        P(),
    )
    return jax.shard_map(per_device, mesh=mesh, in_specs=placed, out_specs=P("chan", None, "tm"), check_vma=False)
```
